128 devices in a mesh: cells: 8 (over y, z_lo), sensors: 16 (over z_hi, x, core).
Axes of the slice: x: 4, y: 4, z: 4 (z_hi: 2, z_lo: 2; z = z_hi * 2 + z_lo), core: 2. Of those that a mesh axis runs over, the one named last changes fastest.
Arguments:
- rhs: float32 [256, 6, 128, 128], P('sensors', None, 'cells'), may hold values from -18 to 18
- forward_map: bfloat16 [2, 128, 128, 16384], P(None, None, 'sensors', 'cells'), may hold values from -0.125 to 0.125
- stiffness: float32 [128, 128], P('cells'), may hold values from 0.5 to 1.5
- reaction: float32 [128, 128], P('cells'), may hold values from 0.25 to 2
- noise_weight: float32 [128], replicated, may hold values from 0.3 to 3
- sensor_cell: int32 [128], replicated, may hold values from 0 to 16383, as said below
Outputs:
- solution: float32 [256, 6, 128, 128], P('sensors', None, 'cells')
- residual: float32 [256, 6, 128, 128], P('sensors', None, 'cells')
The draws below stay inside these ranges and needn't reach their ends.
Inputs may be any that keep to these rules, and one draw needn't show every extreme that they name: `sensor_cell`: row-major index over the 128 x 128 grid of the cell under each sensor; several sensors may share a cell.
All inputs are finite; a program needn't handle non-finite values.
Results may differ from the reference program's by a relative error of at most 0.0073.
Values may be sent and summed in bfloat16 or wider, within the bound.
A program may use at most 128 MiB of HBM per device.

```python
import math
import jax
import jax.numpy as jnp
from jax import lax

SAMPLES = 6
NF = 128
NT = 256
NS = 128
GX = 128
GY = 128
NC = 16384
SWEEPS = 4
ITERS = 2


def draw_sensor_cell(key, part):
    key_cells, key_upper, key_lower = jax.random.split(jax.random.fold_in(key, 17), 3)
    chosen = jax.random.randint(key_cells, (NS,), 0, NC, dtype=jnp.int32)
    upper_slot = jax.random.randint(key_upper, (), 0, NS, dtype=jnp.int32)
    lower_slot = (upper_slot + 1 + jax.random.randint(key_lower, (), 0, NS - 1, dtype=jnp.int32)) % NS
    positions = jnp.arange(NS, dtype=jnp.int32)
    chosen = jnp.where(positions == upper_slot, NC - 1, chosen)
    return jnp.where(positions == lower_slot, 0, chosen).astype(jnp.int32)


def shard_levels(stream_key, extent, pieces, low, largest):
    loudness = 1.0
    for position, parts in pieces:
        heights = jax.random.uniform(jax.random.fold_in(jax.random.fold_in(stream_key, 6), position), (parts,), jnp.float32, low / len(pieces), largest / len(pieces))
        loudness = loudness * jnp.repeat(jnp.exp(heights), extent[position] // parts).reshape((-1,) + (1,) * (len(extent) - 1 - position))
    return loudness


def normal_values(rng, extent, deviation, most, pieces=(), kind=jnp.bfloat16):
    loudness = shard_levels(rng, extent, pieces, -0.22, 0.18) if pieces else 1.0
    drawn = jax.random.normal(rng, extent, jnp.float32) * deviation * loudness
    return jnp.minimum(jnp.maximum(drawn, -most), most).astype(kind)


def setup_inputs(seed: int = 0) -> dict:
    key_list = jax.random.split(jax.random.key(seed), 7)
    return {
        "rhs": normal_values(key_list[0], (NT, SAMPLES, GX, GY), 3.0, 18.0, ((0, 16), (2, 8)), jnp.float32),
        "forward_map": normal_values(key_list[1], (2, NF, NS, NC), (NC // 8) ** -0.5, 0.125, ((2, 16), (3, 8))),
        "stiffness": jnp.clip(jnp.exp(math.log(1.5) - 1.0986123 * jax.random.uniform(key_list[2], (GX, GY), jnp.float32) ** shard_levels(key_list[2], (GX, GY), ((0, 8),), -0.2, 0.2)), 0.5, 1.5),
        "reaction": jnp.clip(jnp.exp(math.log(2.0) - 2.0794415 * jax.random.uniform(key_list[3], (GX, GY), jnp.float32) ** shard_levels(key_list[3], (GX, GY), ((0, 8),), -0.2, 0.2)), 0.25, 2.0),
        "noise_weight": jnp.clip(jnp.exp(jax.random.uniform(key_list[4], (NS,), jnp.float32, math.log(0.3), math.log(3.0))), 0.3, 3.0),
        "sensor_cell": draw_sensor_cell(jax.random.fold_in(key_list[6], 71), 0),
    }


DAMPING = 0.8

def neighbour_sum(field):
    padded = jnp.pad(field, ((0, 0), (0, 0), (1, 1), (1, 1)))
    return padded[:, :, 2:, 1:-1] + padded[:, :, :-2, 1:-1] + padded[:, :, 1:-1, 2:] + padded[:, :, 1:-1, :-2]

def transform_table(freqs, period):
    wave = jnp.arange(freqs, dtype=jnp.int32)[:, None]
    moment = jnp.arange(period, dtype=jnp.int32)[None, :]
    phase = (wave * moment % period).astype(jnp.float32) * (2.0 * math.pi / period)
    factor = 1.0 / math.sqrt(period)
    return jnp.concatenate([jnp.cos(phase) * factor, -jnp.sin(phase) * factor], axis=0).astype(jnp.bfloat16)

def prior_apply(field, stiffness, diagonal):
    return diagonal * field - stiffness * neighbour_sum(stiffness * field)

def precondition(residual, stiffness, diagonal, inverse):
    update = DAMPING * inverse * residual
    for sweep in range(SWEEPS - 1):
        update = update + DAMPING * inverse * (residual - prior_apply(update, stiffness, diagonal))
    return update

def misfit_apply(field, forward_map, noise_weight, sensor_cell, table):
    period = field.shape[0]
    spectrum = jnp.dot(table, field.astype(jnp.bfloat16).reshape(period, -1), preferred_element_type=jnp.float32)
    spectrum = spectrum.astype(jnp.bfloat16).reshape(2 * NF, SAMPLES, NC)
    real_part = spectrum[:NF]
    imag_part = spectrum[NF:]

    def observe(items):
        map_real, map_imag, field_real, field_imag = items
        obs_real = jnp.dot(field_real, map_real.T, preferred_element_type=jnp.float32) - jnp.dot(field_imag, map_imag.T, preferred_element_type=jnp.float32)
        obs_imag = jnp.dot(field_imag, map_real.T, preferred_element_type=jnp.float32) + jnp.dot(field_real, map_imag.T, preferred_element_type=jnp.float32)
        return (obs_real, obs_imag)
    obs_real, obs_imag = lax.map(observe, (forward_map[0], forward_map[1], real_part, imag_part))
    obs_real = obs_real + real_part[:, :, sensor_cell].astype(jnp.float32)
    obs_imag = obs_imag + imag_part[:, :, sensor_cell].astype(jnp.float32)
    weighted_real = (noise_weight * obs_real).astype(jnp.bfloat16)
    weighted_imag = (noise_weight * obs_imag).astype(jnp.bfloat16)

    def spread(items):
        map_real, map_imag, data_real, data_imag = items
        back_real = jnp.dot(data_real, map_real, preferred_element_type=jnp.float32) + jnp.dot(data_imag, map_imag, preferred_element_type=jnp.float32)
        back_imag = jnp.dot(data_imag, map_real, preferred_element_type=jnp.float32) - jnp.dot(data_real, map_imag, preferred_element_type=jnp.float32)
        return (back_real, back_imag)
    back_real, back_imag = lax.map(spread, (forward_map[0], forward_map[1], weighted_real, weighted_imag))
    back_real = back_real.at[:, :, sensor_cell].add(weighted_real.astype(jnp.float32))
    back_imag = back_imag.at[:, :, sensor_cell].add(weighted_imag.astype(jnp.float32))
    adjoint = jnp.concatenate([back_real, back_imag], axis=0).reshape(2 * NF, -1)
    time_terms = jnp.dot(table.astype(jnp.float32).T, adjoint, precision=lax.Precision.HIGHEST, preferred_element_type=jnp.float32)
    return time_terms.reshape(field.shape)

def reference(rhs, forward_map, stiffness, reaction, noise_weight, sensor_cell):
    diagonal = reaction + 4.0 * stiffness * stiffness
    inverse = 1.0 / diagonal
    table = transform_table(NF, NT)
    solution = precondition(rhs, stiffness, diagonal, inverse)
    residual = rhs
    for iteration in range(ITERS):
        hessian = prior_apply(solution, stiffness, diagonal) + misfit_apply(solution, forward_map, noise_weight, sensor_cell, table)
        residual = rhs - hessian
        solution = solution + precondition(residual, stiffness, diagonal, inverse)
    return (solution, residual)
```

```python
import functools
import math

import jax
import jax.numpy as jnp
import numpy as np
from jax import lax
from jax.experimental import pallas as pl
from jax.experimental.pallas import tpu as pltpu
from jax.sharding import PartitionSpec as P

MESH = pl.DeviceIdType.MESH
BF16 = jnp.bfloat16
F32 = jnp.float32
DAMPING = 0.8
ROWS = 16
HALO = 4
EXT = ROWS + 2 * HALO
STEPS = 16
COLS = 128
CELLS = ROWS * COLS
NT = 256
FB = 16
GROUPS = 8
SENS = 8
CHUNK = 2
CHUNKS = 3
JOBS = 2 * CHUNKS


def transform_tables():
    wave = np.arange(128)[:, None]
    moment = np.arange(NT)[None, :]
    phase = (wave * moment % NT).astype(np.float32) * np.float32(2.0 * math.pi / NT)
    factor = np.float32(1.0 / math.sqrt(NT))
    real = (np.cos(phase) * factor).reshape(GROUPS, 1, FB, NT)
    imag = (-np.sin(phase) * factor).reshape(GROUPS, 1, FB, NT)
    return np.concatenate([real, imag], axis=1).reshape(NT, NT)


def kernel(
    rhs_hbm,
    map_hbm,
    stiff_ref,
    react_ref,
    weight_sm,
    cell_sm,
    table_ref,
    table_t_ref,
    sol_ref,
    res_ref,
    gv,
    xg,
    spec,
    adj,
    y,
    rsib,
    rh,
    rx,
    rz,
    ms,
    oall,
    rhs_ext,
    res_ext,
    xf,
    sx,
    qx,
    c_sw,
    c_k,
    c_s,
    c_si,
    c_d,
    ua,
    ub,
    marks,
    nwt,
    loc_sem,
    init_send,
    init_recv,
    ag_send,
    ag_recv,
    sib_send,
    sib_recv,
    rh_send,
    rh_recv,
    rx_send,
    rx_recv,
    rz_send,
    rz_recv,
    o_send,
    o_recv,
    halo_send,
    halo_recv,
):
    c_me = lax.axis_index("cells")
    s_me = lax.axis_index("sensors")
    core = lax.rem(s_me, 2)
    chip = s_me // 2
    xpos = lax.rem(chip, 4)
    zpos = chip // 4

    def sidx(dz, dx, cc):
        return (lax.rem(zpos + dz, 2) * 4 + lax.rem(xpos + dx, 4)) * 2 + cc

    other = 1 - core
    sib = {"sensors": sidx(0, 0, other)}
    xp = {"sensors": sidx(0, 1, core)}
    xm = {"sensors": sidx(0, 3, core)}
    zp = {"sensors": sidx(1, 0, core)}
    cnext = {"cells": lax.rem(c_me + 1, 8)}
    cprev = {"cells": lax.rem(c_me + 7, 8)}

    def rdma(src, dst, ss, rs, dev):
        return pltpu.make_async_remote_copy(
            src_ref=src, dst_ref=dst, send_sem=ss, recv_sem=rs, device_id=dev, device_id_type=MESH
        )

    map_copies = [
        pltpu.make_async_copy(map_hbm.at[p, g], gv.at[p, g], loc_sem.at[p * GROUPS + g])
        for p in range(2)
        for g in range(GROUPS)
    ]
    rhs_copies = [
        pltpu.make_async_copy(
            rhs_hbm.at[b], rhs_ext.at[b, pl.ds(HALO, ROWS)], loc_sem.at[16 + b]
        )
        for b in range(6)
    ]
    for cp in rhs_copies:
        cp.start()
    for cp in map_copies:
        cp.start()

    barrier = pltpu.get_barrier_semaphore()
    peers = [sib, xp, xm, zp] + [{"cells": lax.rem(c_me + j, 8)} for j in range(1, 8)]
    for peer in peers:
        pl.semaphore_signal(barrier, inc=1, device_id=peer, device_id_type=MESH)
    pl.semaphore_wait(barrier, len(peers))

    def coef_copies():
        return [
            rdma(stiff_ref.at[pl.ds(8, 8)], sx.at[pl.ds(0, 8)], init_send.at[0], init_recv.at[0], cnext),
            rdma(stiff_ref.at[pl.ds(0, 8)], sx.at[pl.ds(24, 8)], init_send.at[1], init_recv.at[1], cprev),
            rdma(react_ref.at[pl.ds(8, 8)], qx.at[pl.ds(0, 8)], init_send.at[2], init_recv.at[2], cnext),
            rdma(react_ref.at[pl.ds(0, 8)], qx.at[pl.ds(24, 8)], init_send.at[3], init_recv.at[3], cprev),
        ]

    def halo_copies(ref, k, ssem, rsem):
        bs = pl.ds(k * CHUNK, CHUNK)
        return [
            rdma(
                ref.at[bs, pl.ds(ROWS, HALO)], ref.at[bs, pl.ds(0, HALO)], ssem.at[k, 0], rsem.at[k, 0], cnext
            ),
            rdma(
                ref.at[bs, pl.ds(HALO, HALO)],
                ref.at[bs, pl.ds(HALO + ROWS, HALO)],
                ssem.at[k, 1],
                rsem.at[k, 1],
                cprev,
            ),
        ]

    first = coef_copies()
    for cp in first:
        cp.start()
    for b in range(6):
        rhs_copies[b].wait()
        if b % 2 == 1:
            for cp in halo_copies(rhs_ext, b // 2, halo_send.at[0], halo_recv.at[0]):
                cp.start()

    lane = lax.broadcasted_iota(jnp.int32, (8, COLS), 1)
    acc = jnp.zeros((8, COLS), F32)
    for s in range(SENS):
        acc = jnp.where(lax.rem(lane, 8) == s, weight_sm[s_me * SENS + s], acc)
    nwt[...] = acc
    row = lax.broadcasted_iota(jnp.int32, (16, 512), 0)
    target = jnp.zeros((16, 512), jnp.int32)
    for s in range(SENS):
        target = jnp.where(lax.rem(row, 8) == s, cell_sm[s_me * SENS + s], target)
    for part in range(4):
        cell_id = lax.broadcasted_iota(jnp.int32, (16, 512), 1) + (c_me * CELLS + part * 512)
        marks[:, part * 512 : (part + 1) * 512] = jnp.where(cell_id == target, 1.0, 0.0).astype(BF16)

    sx[8:24, :] = stiff_ref[...]
    qx[8:24, :] = react_ref[...]
    for cp in first:
        cp.wait()
    erow = lax.broadcasted_iota(jnp.int32, (32, COLS), 0) + (c_me * ROWS - 8)
    inside = jnp.logical_and(erow >= 0, erow < 128)
    st = jnp.where(inside, sx[...], 0.0)
    re = jnp.where(inside, qx[...], 1.0)
    dg = re + 4.0 * st * st
    wv = DAMPING / dg
    si = jnp.where(inside, 1.0 / jnp.where(inside, st, 1.0), 0.0)
    for ref, val in ((c_sw, st * wv), (c_k, st * st * wv), (c_s, st), (c_si, si), (c_d, dg)):
        ref[...] = jnp.broadcast_to(val[8 - HALO : 8 - HALO + EXT][:, None, :], (EXT, STEPS, COLS))

    lane_s = lax.broadcasted_iota(jnp.int32, (STEPS, COLS), 1)
    not_first = lane_s > 0
    not_last = lane_s < COLS - 1

    def side_sum(v):
        n = v.shape[0]
        flat = v.reshape(n * STEPS, COLS)
        left = pltpu.roll(flat, 1, 1).reshape(v.shape)
        right = pltpu.roll(flat, COLS - 1, 1).reshape(v.shape)
        return jnp.where(not_first[None], left, 0.0) + jnp.where(not_last[None], right, 0.0)

    def precondition(src, b):
        def put(i, carry):
            rs = pl.ds(i * 4, 4)
            ua[rs] = c_sw[rs] * src[b, rs]
            return carry

        lax.fori_loop(0, EXT // 4, put, 0)
        bufs = [ua, ub, ua]
        for sweep in range(3):
            lo, hi = 1 + sweep, EXT - 1 - sweep
            now = bufs[sweep]

            def stencil(i, carry, now=now, lo=lo, sweep=sweep):
                r0 = lo + i * 2
                rs = pl.ds(r0, 2)
                mid = now[rs]
                nb = now[pl.ds(r0 + 1, 2)] + now[pl.ds(r0 - 1, 2)] + side_sum(mid)
                new = (1.0 - DAMPING) * mid + c_sw[rs] * src[b, rs] + c_k[rs] * nb
                if sweep < 2:
                    bufs[sweep + 1][rs] = new
                else:
                    xr = pl.ds(r0 - 3, 2)
                    xf[b, xr] = xf[b, xr] + c_si[rs] * new
                return carry

            lax.fori_loop(0, (hi - lo) // 2, stencil, 0)

    d_me = s_me

    def chunk_of(dz, dx, cc):
        return sidx(dz, dx, cc)

    def ag_copy(k, idx, dz, dx, cc, half, dev):
        d = chunk_of(dz, dx, cc)
        ref = xg.at[k, d] if half is None else xg.at[k, d, half]
        return rdma(ref, ref, ag_send.at[k, idx], ag_recv.at[k, idx], dev)

    def ag_sends(k):
        return {
            "sib_o": ag_copy(k, 0, 0, 0, core, None, sib),
            "xp_o": ag_copy(k, 1, 0, 0, core, None, xp),
            "xm_o": ag_copy(k, 2, 0, 0, core, None, xm),
            "zp_o": ag_copy(k, 3, 0, 0, core, None, zp),
            "xp_h": ag_copy(k, 4, 0, 3, core, 0, xp),
            "xm_h": ag_copy(k, 5, 0, 1, core, 1, xm),
            "xp_z": ag_copy(k, 6, 1, 0, core, None, xp),
            "xm_z": ag_copy(k, 7, 1, 0, core, None, xm),
            "xp_zh": ag_copy(k, 8, 1, 3, core, 0, xp),
            "xm_zh": ag_copy(k, 9, 1, 1, core, 1, xm),
            "sib_1": ag_copy(k, 10, 0, 3, core, None, sib),
            "sib_2": ag_copy(k, 11, 0, 1, core, None, sib),
            "sib_3": ag_copy(k, 12, 1, 0, core, None, sib),
            "sib_4": ag_copy(k, 13, 0, 2, core, None, sib),
            "sib_5": ag_copy(k, 14, 1, 3, core, None, sib),
            "sib_6": ag_copy(k, 15, 1, 1, core, None, sib),
            "sib_7": ag_copy(k, 16, 1, 2, core, None, sib),
        }

    def a0(u):
        k = lax.rem(u, CHUNKS)
        s = ag_sends(k)
        for name in ("xp_o", "xm_o", "zp_o", "sib_o"):
            s[name].start()

    def a1(u):
        k = lax.rem(u, CHUNKS)
        s = ag_sends(k)
        s["zp_o"].wait_recv()
        s["xp_z"].start()
        s["xm_z"].start()
        s["xp_o"].wait_recv()
        s["xp_h"].start()
        s["xm_o"].wait_recv()
        s["xm_h"].start()
        s["sib_1"].start()
        s["sib_2"].start()
        s["sib_3"].start()

    def a2(u):
        k = lax.rem(u, CHUNKS)
        s = ag_sends(k)
        s["xp_z"].wait_recv()
        s["xp_zh"].start()
        s["xm_z"].wait_recv()
        s["xm_zh"].start()
        s["xp_h"].wait_recv()
        s["xm_h"].wait_recv()
        s["sib_4"].start()
        s["sib_5"].start()
        s["sib_6"].start()

    def a3(u):
        k = lax.rem(u, CHUNKS)
        s = ag_sends(k)
        s["xp_zh"].wait_recv()
        s["xm_zh"].wait_recv()
        s["sib_7"].start()

    def a4(u):
        k = lax.rem(u, CHUNKS)
        s = ag_sends(k)
        for name in ("sib_o", "sib_1", "sib_2", "sib_3", "sib_4", "sib_5", "sib_6", "sib_7"):
            s[name].wait_recv()
        for name in s:
            s[name].wait_send()

    frow = lax.broadcasted_iota(jnp.int32, (FB, COLS), 0)
    fold = frow == lax.broadcasted_iota(jnp.int32, (FB, COLS), 1) // SENS

    def o_copies(u, k):
        return [
            rdma(
                oall.at[u, c_me], oall.at[u, c_me], o_send.at[k, j - 1], o_recv.at[u, j - 1],
                {"cells": lax.rem(c_me + j, 8)},
            )
            for j in range(1, 8)
        ]

    def observe(u):
        k = lax.rem(u, CHUNKS)

        for bb in range(CHUNK):

            def dft(rp, carry, bb=bb):
                x0 = xg[k, :, bb, 2 * rp].reshape(NT, COLS)
                x1 = xg[k, :, bb, 2 * rp + 1].reshape(NT, COLS)
                both = jnp.concatenate([x0, x1], axis=1)
                v = jnp.dot(table_ref[...], both, preferred_element_type=F32).astype(BF16)
                cols = pl.ds(pl.multiple_of(rp * 256, 256), 256)
                spec[:, bb * 32 : bb * 32 + 32, cols] = v.reshape(GROUPS, 32, 256)
                return carry

            lax.fori_loop(0, ROWS // 2, dft, 0)

        def group(g, carry):
            vg = spec[g]
            parts = []
            for p in range(2):
                o = lax.dot_general(
                    vg, gv[p, g], (((1,), (1,)), ((), ())), preferred_element_type=F32
                ).reshape(4, FB, COLS)
                parts.append(jnp.sum(jnp.where(fold[None], o, 0.0), axis=1))
            a, b = parts
            rows = []
            for bb in range(CHUNK):
                rows.append(a[2 * bb : 2 * bb + 1] - b[2 * bb + 1 : 2 * bb + 2])
                rows.append(a[2 * bb + 1 : 2 * bb + 2] + b[2 * bb : 2 * bb + 1])
            oall[u, c_me, g] = jnp.concatenate(rows, axis=0)
            return carry

        lax.fori_loop(0, GROUPS, group, 0)
        for cp in o_copies(u, k):
            cp.start()

    def sib_copies(k):
        out = {}
        for n, dx in enumerate((2, 1, 3, 0)):
            for zr in (1, 0):
                i = n * 2 + zr
                ci = sidx(zr, dx, 0) // 2
                out[(dx, zr)] = rdma(
                    y.at[k, ci * 2 + other], rsib.at[k, ci], sib_send.at[k, i], sib_recv.at[k, i], sib
                )
        return out

    def pull(u):
        k = lax.rem(u, CHUNKS)
        for cp in o_copies(u, k):
            cp.wait_recv()

        def group(g, carry):
            tot = oall[u, 0, g]
            for c in range(1, 8):
                tot = tot + oall[u, c, g]
            w = nwt[0:4] * tot
            rows = []
            for bb in range(CHUNK):
                wr = jnp.broadcast_to(w[2 * bb : 2 * bb + 1], (FB, COLS))
                wi = jnp.broadcast_to(w[2 * bb + 1 : 2 * bb + 2], (FB, COLS))
                wr = jnp.where(fold, wr, 0.0)
                wi = jnp.where(fold, wi, 0.0)
                rows.append(jnp.concatenate([wr, wi], axis=1))
                rows.append(jnp.concatenate([wi, -wr], axis=1))
            wm = jnp.concatenate(rows, axis=0).astype(BF16)
            for part in range(4):
                cols = slice(part * 512, part * 512 + 512)
                gg = jnp.concatenate([gv[0, g, :, cols], gv[1, g, :, cols]], axis=0)
                a = jnp.dot(wm, gg, preferred_element_type=F32).astype(BF16)
                jr = pl.ds(pl.multiple_of(g * 32, 32), 32)
                for bb in range(CHUNK):
                    adj[bb, jr, cols] = a[bb * 32 : bb * 32 + 32]
            return carry

        lax.fori_loop(0, GROUPS, group, 0)
        for bb in range(CHUNK):

            def idft(rp, carry, bb=bb):
                cols = pl.ds(pl.multiple_of(rp * 256, 256), 256)
                v = jnp.dot(table_t_ref[...], adj[bb, :, cols], preferred_element_type=F32).astype(BF16)
                y[k, :, bb, 2 * rp] = v[:, :COLS].reshape(16, STEPS, COLS)
                y[k, :, bb, 2 * rp + 1] = v[:, COLS:].reshape(16, STEPS, COLS)
                return carry

            lax.fori_loop(0, ROWS // 2, idft, 0)
        for cp in sib_copies(k).values():
            cp.start()

    def add_into(terms, out, dtype):
        for bb in range(CHUNK):

            def body(i, carry, bb=bb):
                rs = pl.ds(i * 4, 4)
                tot = None
                for t in terms:
                    if t[1] is None or t[1] == bb:
                        v = t[0](bb, rs).astype(F32)
                        tot = v if tot is None else tot + v
                out(bb, rs, tot.astype(dtype))
                return carry

            lax.fori_loop(0, ROWS // 4, body, 0)

    def rh_copies(k, ci, zr):
        d = ci * 2 + core
        return (
            rdma(y.at[k, d, 0], rh.at[k, 0, zr], rh_send.at[k, zr], rh_recv.at[k, zr], xp),
            rdma(y.at[k, d, 1], rh.at[k, 1, zr], rh_send.at[k, 2 + zr], rh_recv.at[k, 2 + zr], xm),
        )

    def rx_copy(k, ci, zr, side):
        d = ci * 2 + core
        i = side * 2 + zr
        return rdma(y.at[k, d], rx.at[k, side, zr], rx_send.at[k, i], rx_recv.at[k, i], (xp, xm)[side])

    def rz_copy(k):
        d = sidx(1, 0, 0) + core
        return rdma(y.at[k, d], rz.at[k], rz_send.at[k], rz_recv.at[k], zp)

    def yset(k, d):
        def out(bb, rs, v):
            y[k, d, bb, rs] = v

        return out

    def r1(u):
        k = lax.rem(u, CHUNKS)
        sc = sib_copies(k)
        for zr in (1, 0):
            ci = sidx(zr, 2, 0) // 2
            d = ci * 2 + core
            sc[(2, zr)].wait_recv()
            add_into(
                [(lambda bb, rs, d=d: y[k, d, bb, rs], None), (lambda bb, rs, ci=ci: rsib[k, ci, bb, rs], None)],
                yset(k, d),
                BF16,
            )
            for cp in rh_copies(k, ci, zr):
                cp.start()

    def r2(u):
        k = lax.rem(u, CHUNKS)
        sc = sib_copies(k)
        for zr in (1, 0):
            for side, dx in ((0, 1), (1, 3)):
                ci = sidx(zr, dx, 0) // 2
                d = ci * 2 + core
                sc[(dx, zr)].wait_recv()
                rh_copies(k, ci, zr)[side].wait_recv()
                add_into(
                    [
                        (lambda bb, rs, d=d: y[k, d, bb, rs], None),
                        (lambda bb, rs, ci=ci: rsib[k, ci, bb, rs], None),
                        (lambda bb, rs, side=side, zr=zr: rh[k, side, zr, rs], side),
                    ],
                    yset(k, d),
                    BF16,
                )
                rx_copy(k, ci, zr, side).start()

    def r3(u):
        k = lax.rem(u, CHUNKS)
        sc = sib_copies(k)

        def mset(bb, rs, v):
            ms[bb, rs] = v

        for zr in (1, 0):
            ci = sidx(zr, 0, 0) // 2
            d = ci * 2 + core
            sc[(0, zr)].wait_recv()
            rx_copy(k, ci, zr, 0).wait_recv()
            rx_copy(k, ci, zr, 1).wait_recv()
            add_into(
                [
                    (lambda bb, rs, d=d: y[k, d, bb, rs], None),
                    (lambda bb, rs, ci=ci: rsib[k, ci, bb, rs], None),
                    (lambda bb, rs, zr=zr: rx[k, 0, zr, bb, rs], None),
                    (lambda bb, rs, zr=zr: rx[k, 1, zr, bb, rs], None),
                ],
                yset(k, d) if zr == 1 else mset,
                BF16 if zr == 1 else F32,
            )
            if zr == 1:
                rz_copy(k).start()

    def r4(u):
        k = lax.rem(u, CHUNKS)
        rz_copy(k).wait_recv()
        for bb in range(CHUNK):
            b = k * CHUNK + bb

            def body(i, carry, b=b, bb=bb):
                er = pl.ds(HALO + i * 2, 2)
                rs = pl.ds(i * 2, 2)
                mid = xf[b, pl.ds(i * 2 + 1, 2)]
                um = c_s[er] * mid
                up = c_s[pl.ds(HALO + i * 2 - 1, 2)] * xf[b, rs]
                dn = c_s[pl.ds(HALO + i * 2 + 1, 2)] * xf[b, pl.ds(i * 2 + 2, 2)]
                prior = c_d[er] * mid - c_s[er] * (up + dn + side_sum(um))
                m = ms[bb, rs] + rz[k, bb, rs].astype(F32)
                r = rhs_ext[b, er] - (prior + m)
                res_ext[b, er] = r
                res_ref[b, rs] = r
                return carry

            lax.fori_loop(0, ROWS // 2, body, 0)
        for cp in halo_copies(res_ext, k, halo_send.at[1], halo_recv.at[1]):
            cp.start()
        for cp in sib_copies(k).values():
            cp.wait_send()
        for zr in (1, 0):
            for cp in rh_copies(k, 0, zr):
                cp.wait_send()
            for side in range(2):
                rx_copy(k, 0, zr, side).wait_send()
        rz_copy(k).wait_send()
        for cp in o_copies(u, k):
            cp.wait_send()

    def own_to_gather(k):
        for bb in range(CHUNK):
            b = k * CHUNK + bb

            def body(i, carry, b=b, bb=bb):
                xg[k, d_me, bb, pl.ds(i * 4, 4)] = xf[b, pl.ds(1 + i * 4, 4)].astype(BF16)
                return carry

            lax.fori_loop(0, ROWS // 4, body, 0)

    def begin(k):
        for cp in halo_copies(rhs_ext, k, halo_send.at[0], halo_recv.at[0]):
            cp.wait()
        for bb in range(CHUNK):
            b = k * CHUNK + bb
            xf[b] = jnp.zeros((ROWS + 2, STEPS, COLS), F32)
            precondition(rhs_ext, b)

    def update(k):
        for cp in halo_copies(res_ext, k, halo_send.at[1], halo_recv.at[1]):
            cp.wait()

        def body(bb, carry):
            precondition(res_ext, k * CHUNK + bb)
            return carry

        lax.fori_loop(0, CHUNK, body, 0)

    def finish_map():
        for cp in map_copies:
            cp.wait()

        def body(i, carry):
            rs = pl.ds(pl.multiple_of(lax.rem(i, 8) * 16, 16), 16)
            g = i // 8
            gv[0, g, rs] = gv[0, g, rs] + marks[...]
            return carry

        lax.fori_loop(0, 64, body, 0)

    def when_job(u, fn):
        @pl.when(jnp.logical_and(u >= 0, u < JOBS))
        def _():
            fn(u)

    def step(t, carry):
        when_job(t - 2, r1)

        @pl.when(t < CHUNKS)
        def _():
            begin(t)

        @pl.when(t >= CHUNKS)
        def _():
            update(lax.rem(t, CHUNKS))

        @pl.when(t < JOBS)
        def _():
            own_to_gather(lax.rem(t, CHUNKS))
            a0(t)

        @pl.when(t == 0)
        def _():
            finish_map()

        when_job(t - 1, observe)
        when_job(t - 2, r2)
        when_job(t, a1)
        when_job(t - 2, r3)
        when_job(t, a2)
        when_job(t - 1, pull)
        when_job(t - 2, r4)
        when_job(t, a3)
        when_job(t, a4)
        return carry

    lax.fori_loop(0, JOBS + CHUNKS, step, 0)

    def put_out(b, carry):
        sol_ref[b] = xf[b, pl.ds(1, ROWS)]
        return carry

    lax.fori_loop(0, 6, put_out, 0)


def shards(rhs, forward_map, stiffness, reaction, noise_weight, sensor_cell):
    table = transform_tables()
    rhs_t = jnp.transpose(rhs, (1, 2, 0, 3))
    maps = forward_map.reshape(2, GROUPS, FB * SENS, CELLS)
    vm = pl.BlockSpec(memory_space=pltpu.VMEM)
    sm = pl.BlockSpec(memory_space=pltpu.SMEM)
    hb = pl.BlockSpec(memory_space=pl.ANY)
    block = (CHUNK, ROWS, STEPS, COLS)
    dma = pltpu.SemaphoreType.DMA
    out = jax.ShapeDtypeStruct((6, ROWS, STEPS, COLS), F32)
    scratch = [
        pltpu.VMEM((2, GROUPS, FB * SENS, CELLS), BF16),
        pltpu.VMEM((CHUNKS, 16) + block, BF16),
        pltpu.VMEM((GROUPS, 64, CELLS), BF16),
        pltpu.VMEM((CHUNK, NT, CELLS), BF16),
        pltpu.VMEM((CHUNKS, 16) + block, BF16),
        pltpu.VMEM((CHUNKS, 8) + block, BF16),
        pltpu.VMEM((CHUNKS, 2, 2) + block[1:], BF16),
        pltpu.VMEM((CHUNKS, 2, 2) + block, BF16),
        pltpu.VMEM((CHUNKS,) + block, BF16),
        pltpu.VMEM(block, F32),
        pltpu.VMEM((JOBS, 8, GROUPS, 4, COLS), F32),
        pltpu.VMEM((6, EXT, STEPS, COLS), F32),
        pltpu.VMEM((6, EXT, STEPS, COLS), F32),
        pltpu.VMEM((6, ROWS + 2, STEPS, COLS), F32),
        pltpu.VMEM((32, COLS), F32),
        pltpu.VMEM((32, COLS), F32),
        pltpu.VMEM((EXT, STEPS, COLS), F32),
        pltpu.VMEM((EXT, STEPS, COLS), F32),
        pltpu.VMEM((EXT, STEPS, COLS), F32),
        pltpu.VMEM((EXT, STEPS, COLS), F32),
        pltpu.VMEM((EXT, STEPS, COLS), F32),
        pltpu.VMEM((EXT, STEPS, COLS), F32),
        pltpu.VMEM((EXT, STEPS, COLS), F32),
        pltpu.VMEM((16, CELLS), BF16),
        pltpu.VMEM((8, COLS), F32),
        dma((22,)),
        dma((4,)),
        dma((4,)),
        dma((CHUNKS, 17)),
        dma((CHUNKS, 17)),
        dma((CHUNKS, 8)),
        dma((CHUNKS, 8)),
        dma((CHUNKS, 4)),
        dma((CHUNKS, 4)),
        dma((CHUNKS, 4)),
        dma((CHUNKS, 4)),
        dma((CHUNKS,)),
        dma((CHUNKS,)),
        dma((CHUNKS, 7)),
        dma((JOBS, 7)),
        dma((2, CHUNKS, 2)),
        dma((2, CHUNKS, 2)),
    ]
    sol, res = pl.pallas_call(
        kernel,
        out_shape=(out, out),
        in_specs=[hb, hb, vm, vm, sm, sm, vm, vm],
        out_specs=(vm, vm),
        scratch_shapes=scratch,
        compiler_params=pltpu.CompilerParams(
            collective_id=0, has_side_effects=True, vmem_limit_bytes=60 * 1024 * 1024
        ),
    )(
        rhs_t,
        maps,
        stiffness,
        reaction,
        noise_weight,
        sensor_cell,
        jnp.asarray(table, BF16),
        jnp.asarray(table.T, BF16),
    )
    return (jnp.transpose(sol, (2, 0, 1, 3)), jnp.transpose(res, (2, 0, 1, 3)))


def solution(mesh):
    placed = (
        P("sensors", None, "cells", None),
        P(None, None, "sensors", "cells"),
        P("cells", None),
        P("cells", None),
        P(),
        P(),
    )
    return jax.shard_map(
        shards,
        mesh=mesh,
        in_specs=placed,
        out_specs=(P("sensors", None, "cells", None), P("sensors", None, "cells", None)),
        check_vma=False,
    )
```

```python
import functools
import math

import jax
import jax.numpy as jnp
import numpy as np
from jax import lax
from jax.experimental import pallas as pl
from jax.experimental.pallas import tpu as pltpu
from jax.sharding import PartitionSpec as P

MESH = pl.DeviceIdType.MESH
BF16 = jnp.bfloat16
F32 = jnp.float32
DAMPING = 0.8
ROWS = 16
HALO = 4
EXT = ROWS + 2 * HALO
STEPS = 16
COLS = 128
CELLS = ROWS * COLS
NT = 256
FB = 16
GROUPS = 8
SENS = 8
CHUNK = 1
CHUNKS = 6 // CHUNK
SPLIT = 8
FIRST = pl.ds(0, SPLIT)
REST = pl.ds(SPLIT, ROWS - SPLIT)
ORDER = (
    ("update", 0), ("a2", 2), ("a0", 0), ("a1", 1), ("pull", 3), ("r3", 5),
    ("a3", 2), ("observe", 2), ("r2", 4), ("r1", 3),
)
JOBS = 2 * CHUNKS


def transform_tables():
    wave = np.arange(128)[:, None]
    moment = np.arange(NT)[None, :]
    phase = (wave * moment % NT).astype(np.float32) * np.float32(2.0 * math.pi / NT)
    factor = np.float32(1.0 / math.sqrt(NT))
    real = (np.cos(phase) * factor).reshape(GROUPS, 1, FB, NT)
    imag = (-np.sin(phase) * factor).reshape(GROUPS, 1, FB, NT)
    return np.concatenate([real, imag], axis=1).reshape(NT, NT)


def kernel(
    rhs_hbm,
    map_hbm,
    stiff_ref,
    react_ref,
    weight_sm,
    cell_sm,
    table_ref,
    table_t_ref,
    sol_ref,
    res_ref,
    gv,
    xg,
    spec,
    adj,
    y,
    rsib,
    rzf,
    rxg,
    rxf,
    rzg,
    oall,
    rhs_ext,
    res_ext,
    xf,
    sx,
    qx,
    c_sw,
    c_k,
    c_s,
    c_si,
    c_d,
    marks,
    nwt,
    loc_sem,
    init_send,
    init_recv,
    ag_send,
    ag_recv,
    sib_send,
    sib_recv,
    rzf_send,
    rzf_recv,
    rxg_send,
    rxg_recv,
    rxf_send,
    rxf_recv,
    rzg_send,
    rzg_recv,
    o_send,
    o_recv,
    halo_send,
    halo_recv,
):
    c_me = lax.axis_index("cells")
    s_me = lax.axis_index("sensors")
    core = lax.rem(s_me, 2)
    chip = s_me // 2
    xpos = lax.rem(chip, 4)
    zpos = chip // 4

    def sidx(dz, dx, cc):
        return (lax.rem(zpos + dz, 2) * 4 + lax.rem(xpos + dx, 4)) * 2 + cc

    other = 1 - core
    sib = {"sensors": sidx(0, 0, other)}
    xp = {"sensors": sidx(0, 1, core)}
    xm = {"sensors": sidx(0, 3, core)}
    zp = {"sensors": sidx(1, 0, core)}
    xd = {"sensors": sidx(0, 2, core)}
    xto = {1: xp, 2: xd, 3: xm}
    cnext = {"cells": lax.rem(c_me + 1, 8)}
    cprev = {"cells": lax.rem(c_me + 7, 8)}

    def rdma(src, dst, ss, rs, dev):
        return pltpu.make_async_remote_copy(
            src_ref=src, dst_ref=dst, send_sem=ss, recv_sem=rs, device_id=dev, device_id_type=MESH
        )

    map_copies = [
        pltpu.make_async_copy(map_hbm.at[p, g], gv.at[p, g], loc_sem.at[p * GROUPS + g])
        for p in range(2)
        for g in range(GROUPS)
    ]
    rhs_copies = [
        pltpu.make_async_copy(
            rhs_hbm.at[b], rhs_ext.at[b, pl.ds(HALO, ROWS)], loc_sem.at[16 + b]
        )
        for b in range(6)
    ]
    for cp in rhs_copies:
        cp.start()
    for cp in map_copies:
        cp.start()

    barrier = pltpu.get_barrier_semaphore()
    peers = [sib, xp, xm, xd, zp] + [{"cells": lax.rem(c_me + j, 8)} for j in range(1, 8)]
    for peer in peers:
        pl.semaphore_signal(barrier, inc=1, device_id=peer, device_id_type=MESH)
    pl.semaphore_wait(barrier, len(peers))

    def coef_copies():
        return [
            rdma(stiff_ref.at[pl.ds(8, 8)], sx.at[pl.ds(0, 8)], init_send.at[0], init_recv.at[0], cnext),
            rdma(stiff_ref.at[pl.ds(0, 8)], sx.at[pl.ds(24, 8)], init_send.at[1], init_recv.at[1], cprev),
            rdma(react_ref.at[pl.ds(8, 8)], qx.at[pl.ds(0, 8)], init_send.at[2], init_recv.at[2], cnext),
            rdma(react_ref.at[pl.ds(0, 8)], qx.at[pl.ds(24, 8)], init_send.at[3], init_recv.at[3], cprev),
        ]

    def halo_copies(ref, k, ssem, rsem):
        bs = pl.ds(k * CHUNK, CHUNK)
        return [
            rdma(
                ref.at[bs, pl.ds(ROWS, HALO)], ref.at[bs, pl.ds(0, HALO)], ssem.at[k, 0], rsem.at[k, 0], cnext
            ),
            rdma(
                ref.at[bs, pl.ds(HALO, HALO)],
                ref.at[bs, pl.ds(HALO + ROWS, HALO)],
                ssem.at[k, 1],
                rsem.at[k, 1],
                cprev,
            ),
        ]

    first = coef_copies()
    for cp in first:
        cp.start()
    for b in range(6):
        rhs_copies[b].wait()
        if b % CHUNK == CHUNK - 1:
            for cp in halo_copies(rhs_ext, b // CHUNK, halo_send.at[0], halo_recv.at[0]):
                cp.start()

    lane = lax.broadcasted_iota(jnp.int32, (8, COLS), 1)
    acc = jnp.zeros((8, COLS), F32)
    for s in range(SENS):
        acc = jnp.where(lax.rem(lane, 8) == s, weight_sm[s_me * SENS + s], acc)
    nwt[...] = acc
    row = lax.broadcasted_iota(jnp.int32, (16, 512), 0)
    target = jnp.zeros((16, 512), jnp.int32)
    for s in range(SENS):
        target = jnp.where(lax.rem(row, 8) == s, cell_sm[s_me * SENS + s], target)
    for part in range(4):
        cell_id = lax.broadcasted_iota(jnp.int32, (16, 512), 1) + (c_me * CELLS + part * 512)
        marks[:, part * 512 : (part + 1) * 512] = jnp.where(cell_id == target, 1.0, 0.0).astype(BF16)

    sx[8:24, :] = stiff_ref[...]
    qx[8:24, :] = react_ref[...]
    for cp in first:
        cp.wait()
    erow = lax.broadcasted_iota(jnp.int32, (32, COLS), 0) + (c_me * ROWS - 8)
    inside = jnp.logical_and(erow >= 0, erow < 128)
    st = jnp.where(inside, sx[...], 0.0)
    re = jnp.where(inside, qx[...], 1.0)
    dg = re + 4.0 * st * st
    wv = DAMPING / dg
    si = jnp.where(inside, 1.0 / jnp.where(inside, st, 1.0), 0.0)
    for ref, val in ((c_sw, st * wv), (c_k, st * st * wv), (c_s, st), (c_si, si), (c_d, dg)):
        ref[...] = jnp.broadcast_to(val[8 - HALO : 8 - HALO + EXT][:, None, :], (EXT, STEPS, COLS))

    lane_s = lax.broadcasted_iota(jnp.int32, (STEPS, COLS), 1)
    not_first = lane_s > 0
    not_last = lane_s < COLS - 1

    def sides(v):
        left = pltpu.roll(v, 1, 1)
        right = pltpu.roll(v, COLS - 1, 1)
        return jnp.where(not_first, left, 0.0) + jnp.where(not_last, right, 0.0)

    def precondition(src, b, mode):
        levels = [{}, {}, {}]
        first = {}
        for r in range(EXT + 3):
            if r < EXT:
                first[r] = c_sw[r] * src[b, r]
                levels[0][r] = first[r]
            for n in range(3):
                q = r - 1 - n
                if not n + 1 <= q <= EXT - 2 - n:
                    continue
                now = levels[n]
                nb = now[q - 1] + now[q + 1] + sides(now[q])
                new = (1.0 - DAMPING) * now[q] + first[q] + c_k[q] * nb
                if n < 2:
                    levels[n + 1][q] = new
                elif mode == 0:
                    xf[b, q - 3] = c_si[q] * new
                elif mode == 1:
                    xf[b, q - 3] = xf[b, q - 3] + c_si[q] * new
                elif HALO <= q < HALO + ROWS:
                    sol_ref[b, q - HALO] = xf[b, q - 3] + c_si[q] * new

    d_me = s_me

    def ag_copy(k, idx, dz, dx, rows, dev):
        d = sidx(dz, dx, core)
        ref = xg.at[k, d] if rows is None else xg.at[k, d, :, rows]
        return rdma(ref, ref, ag_send.at[k, idx], ag_recv.at[k, idx], dev)

    def ag_copies(k):
        table = [
            (0, 0, None, sib),
            (0, 0, None, xp),
            (0, 0, None, xm),
            (0, 0, None, xd),
            (0, 0, None, zp),
            (1, 0, REST, xp),
            (1, 0, REST, xm),
            (1, 0, REST, xd),
            (0, 3, FIRST, zp),
            (0, 1, FIRST, zp),
            (0, 2, FIRST, zp),
            (0, 3, None, sib),
            (0, 1, None, sib),
            (0, 2, None, sib),
            (1, 0, None, sib),
            (1, 3, None, sib),
            (1, 1, None, sib),
            (1, 2, None, sib),
        ]
        return [ag_copy(k, i, *row) for i, row in enumerate(table)]

    def a0(u):
        k = lax.rem(u, CHUNKS)
        own_to_gather(k)
        s = ag_copies(k)
        for i in (4, 1, 2, 3, 0):
            s[i].start()

    def a1(u):
        s = ag_copies(lax.rem(u, CHUNKS))
        s[4].wait_recv()
        for i in (5, 6, 7, 14):
            s[i].start()
        for i, z, f in ((1, 8, 11), (2, 9, 12), (3, 10, 13)):
            s[i].wait_recv()
            s[z].start()
            s[f].start()

    def a2(u):
        s = ag_copies(lax.rem(u, CHUNKS))
        for i, z, f in ((5, 8, 15), (6, 9, 16), (7, 10, 17)):
            s[i].wait_recv()
            s[z].wait_recv()
            s[f].start()

    def a3(u):
        s = ag_copies(lax.rem(u, CHUNKS))
        for i in (0, 11, 12, 13, 14, 15, 16, 17):
            s[i].wait_recv()
        for cp in s:
            cp.wait_send()

    frow = lax.broadcasted_iota(jnp.int32, (FB, COLS), 0)
    fold = frow == lax.broadcasted_iota(jnp.int32, (FB, COLS), 1) // SENS

    def o_copies(u, k):
        return [
            rdma(
                oall.at[u, c_me], oall.at[u, c_me], o_send.at[k, j - 1], o_recv.at[u, j - 1],
                {"cells": lax.rem(c_me + j, 8)},
            )
            for j in range(1, 8)
        ]

    def observe(u):
        k = lax.rem(u, CHUNKS)

        for bb in range(CHUNK):

            def dft(rp, carry, bb=bb):
                x0 = xg[k, :, bb, 2 * rp].reshape(NT, COLS)
                x1 = xg[k, :, bb, 2 * rp + 1].reshape(NT, COLS)
                both = jnp.concatenate([x0, x1], axis=1)
                v = jnp.dot(table_ref[...], both, preferred_element_type=F32).astype(BF16)
                cols = pl.ds(pl.multiple_of(rp * 256, 256), 256)
                spec[:, bb * 32 : bb * 32 + 32, cols] = v.reshape(GROUPS, 32, 256)
                return carry

            lax.fori_loop(0, ROWS // 2, dft, 0, unroll=8)

        def group(g, carry):
            vg = spec[g]
            parts = []
            for p in range(2):
                o = lax.dot_general(
                    vg, gv[p, g], (((1,), (1,)), ((), ())), preferred_element_type=F32
                ).reshape(2 * CHUNK, FB, COLS)
                parts.append(jnp.sum(jnp.where(fold[None], o, 0.0), axis=1))
            a, b = parts
            rows = []
            for bb in range(CHUNK):
                rows.append(a[2 * bb : 2 * bb + 1] - b[2 * bb + 1 : 2 * bb + 2])
                rows.append(a[2 * bb + 1 : 2 * bb + 2] + b[2 * bb : 2 * bb + 1])
            oall[u, c_me, g] = jnp.concatenate(rows, axis=0)
            return carry

        lax.fori_loop(0, GROUPS, group, 0, unroll=4)
        for cp in o_copies(u, k):
            cp.start()

    def sib_copy(k):
        return rdma(y.at[k, other], rsib.at[k], sib_send.at[k], sib_recv.at[k], sib)

    def pull(u):
        k = lax.rem(u, CHUNKS)
        for cp in o_copies(u, k):
            cp.wait_recv()

        def group(g, carry):
            tot = oall[u, 0, g]
            for c in range(1, 8):
                tot = tot + oall[u, c, g]
            w = nwt[0 : 2 * CHUNK] * tot
            rows = []
            for bb in range(CHUNK):
                wr = jnp.broadcast_to(w[2 * bb : 2 * bb + 1], (FB, COLS))
                wi = jnp.broadcast_to(w[2 * bb + 1 : 2 * bb + 2], (FB, COLS))
                wr = jnp.where(fold, wr, 0.0)
                wi = jnp.where(fold, wi, 0.0)
                rows.append(jnp.concatenate([wr, wi], axis=1))
                rows.append(jnp.concatenate([wi, -wr], axis=1))
            wm = jnp.concatenate(rows, axis=0).astype(BF16)
            for part in range(4):
                cols = slice(part * 512, part * 512 + 512)
                gg = jnp.concatenate([gv[0, g, :, cols], gv[1, g, :, cols]], axis=0)
                a = jnp.dot(wm, gg, preferred_element_type=F32).astype(BF16)
                jr = pl.ds(pl.multiple_of(g * 32, 32), 32)
                for bb in range(CHUNK):
                    adj[bb, jr, cols] = a[bb * 32 : bb * 32 + 32]
            return carry

        lax.fori_loop(0, GROUPS, group, 0, unroll=4)
        for bb in range(CHUNK):

            def idft(rp, carry, bb=bb):
                cols = pl.ds(pl.multiple_of(rp * 256, 256), 256)
                v = jnp.dot(table_t_ref[...], adj[bb, :, cols], preferred_element_type=F32).astype(BF16)
                for half in range(2):
                    w = v[:, half * COLS : half * COLS + COLS].reshape(8, 2, STEPS, COLS)
                    for c in range(2):
                        y[k, c, :, bb, 2 * rp + half] = w[:, c]
                return carry

            lax.fori_loop(0, ROWS // 2, idft, 0, unroll=8)
        sib_copy(k).start()

    def block(zr, dx):
        return sidx(zr, dx, 0) // 2

    def total(k, zr, dx, bb, rs, arrived):
        ci = block(zr, dx)
        tot = y[k, core, ci, bb, rs].astype(F32) + rsib[k, ci, bb, rs].astype(F32)
        for ref in arrived:
            tot = tot + ref[bb, rs].astype(F32)
        return tot

    def add_rows(k, zr, dx, lo, hi, arrived):
        for bb in range(CHUNK):
            for r in range(lo, hi, 2):
                rs = pl.ds(r, 2)
                y[k, core, block(zr, dx), bb, rs] = total(k, zr, dx, bb, rs, arrived).astype(BF16)

    def rzf_copy(k, dx):
        return rdma(
            y.at[k, core, block(1, dx), :, FIRST], rzf.at[k, dx, :, FIRST], rzf_send.at[k, dx], rzf_recv.at[k, dx], zp
        )

    def rxg_copy(k, zr, dx):
        i = zr * 3 + dx - 1
        return rdma(
            y.at[k, core, block(zr, dx), :, REST], rxg.at[k, i, :, REST], rxg_send.at[k, i], rxg_recv.at[k, i], xto[dx]
        )

    def rxf_copy(k, dx):
        i = dx - 1
        return rdma(
            y.at[k, core, block(0, dx), :, FIRST], rxf.at[k, i, :, FIRST], rxf_send.at[k, i], rxf_recv.at[k, i], xto[dx]
        )

    def rzg_copy(k):
        return rdma(
            y.at[k, core, block(1, 0), :, REST], rzg.at[k, :, REST], rzg_send.at[k], rzg_recv.at[k], zp
        )

    def r1(u):
        k = lax.rem(u, CHUNKS)
        sib_copy(k).wait_recv()
        for dx in (2, 1, 3):
            add_rows(k, 1, dx, 0, SPLIT, ())
            rzf_copy(k, dx).start()
            add_rows(k, 1, dx, SPLIT, ROWS, ())
            rxg_copy(k, 1, dx).start()
        add_rows(k, 1, 0, 0, SPLIT, ())
        rzf_copy(k, 0).start()
        for dx in (2, 1, 3):
            add_rows(k, 0, dx, SPLIT, ROWS, ())
            rxg_copy(k, 0, dx).start()

    def r2(u):
        k = lax.rem(u, CHUNKS)
        for dx in (2, 1, 3):
            rzf_copy(k, dx).wait_recv()
            add_rows(k, 0, dx, 0, SPLIT, (rzf.at[k, dx],))
            rxf_copy(k, dx).start()
        for dx in (1, 3, 2):
            rxg_copy(k, 1, dx).wait_recv()
        add_rows(k, 1, 0, SPLIT, ROWS, [rxg.at[k, 3 + i] for i in range(3)])
        rzg_copy(k).start()

    def r3(u):
        k = lax.rem(u, CHUNKS)
        rzf_copy(k, 0).wait_recv()
        for dx in (1, 3, 2):
            rxg_copy(k, 0, dx).wait_recv()
            rxf_copy(k, dx).wait_recv()
        rzg_copy(k).wait_recv()
        for bb in range(CHUNK):
            b = k * CHUNK + bb
            for i in range(0, ROWS, 2):
                er = pl.ds(HALO + i, 2)
                rs = pl.ds(i, 2)
                us = [c_s[HALO + i - 1 + n] * xf[b, i + n] for n in range(4)]
                if i < SPLIT:
                    arrived = [rzf.at[k, 0]] + [rxf.at[k, n] for n in range(3)]
                else:
                    arrived = [rzg.at[k]] + [rxg.at[k, n] for n in range(3)]
                m = total(k, 0, 0, bb, rs, arrived)
                for n in range(2):
                    e = HALO + i + n
                    nb = us[n] + us[n + 2] + sides(us[n + 1])
                    prior = c_d[e] * xf[b, i + n + 1] - c_s[e] * nb
                    r = rhs_ext[b, e] - (prior + m[n])
                    res_ext[b, e] = r
                    res_ref[b, i + n] = r
        for cp in halo_copies(res_ext, k, halo_send.at[1], halo_recv.at[1]):
            cp.start()
        sib_copy(k).wait_send()
        for dx in range(4):
            rzf_copy(k, dx).wait_send()
        for dx in (1, 2, 3):
            rxf_copy(k, dx).wait_send()
            for zr in range(2):
                rxg_copy(k, zr, dx).wait_send()
        rzg_copy(k).wait_send()
        for cp in o_copies(u, k):
            cp.wait_send()

    def own_to_gather(k):
        for bb in range(CHUNK):
            b = k * CHUNK + bb

            def body(i, carry, b=b, bb=bb):
                xg[k, d_me, bb, pl.ds(i * 4, 4)] = xf[b, pl.ds(1 + i * 4, 4)].astype(BF16)
                return carry

            lax.fori_loop(0, ROWS // 4, body, 0, unroll=4)

    def begin(k):
        for cp in halo_copies(rhs_ext, k, halo_send.at[0], halo_recv.at[0]):
            cp.wait()
        for bb in range(CHUNK):
            b = k * CHUNK + bb
            precondition(rhs_ext, b, 0)

    def update(k, mode):
        for cp in halo_copies(res_ext, k, halo_send.at[1], halo_recv.at[1]):
            cp.wait()

        for bb in range(CHUNK):
            precondition(res_ext, k * CHUNK + bb, mode)

    def finish_map():
        for cp in map_copies:
            cp.wait()

        def body(i, carry):
            rs = pl.ds(pl.multiple_of(lax.rem(i, 8) * 16, 16), 16)
            g = i // 8
            gv[0, g, rs] = gv[0, g, rs] + marks[...]
            return carry

        lax.fori_loop(0, 64, body, 0, unroll=4)

    def advance(u):
        @pl.when(u < CHUNKS)
        def _():
            begin(u)

        @pl.when(jnp.logical_and(u >= CHUNKS, u < JOBS))
        def _():
            update(lax.rem(u, CHUNKS), 1)

        @pl.when(u >= JOBS)
        def _():
            update(lax.rem(u, CHUNKS), 2)

    stages = {
        "a0": a0, "a1": a1, "a2": a2, "a3": a3, "observe": observe, "pull": pull, "r1": r1, "r2": r2, "r3": r3
    }

    def step(t, carry):
        for name, late in ORDER:
            u = t - late
            if name == "update":
                advance(u)
                continue

            @pl.when(jnp.logical_and(u >= 0, u < JOBS))
            def _(name=name, u=u):
                stages[name](u)

            if name == "a0":

                @pl.when(t == 1)
                def _():
                    finish_map()

        return carry

    lax.fori_loop(0, JOBS + CHUNKS, step, 0)


def shards(rhs, forward_map, stiffness, reaction, noise_weight, sensor_cell):
    table = transform_tables()
    rhs_t = jnp.transpose(rhs, (1, 2, 0, 3))
    maps = forward_map.reshape(2, GROUPS, FB * SENS, CELLS)
    vm = pl.BlockSpec(memory_space=pltpu.VMEM)
    sm = pl.BlockSpec(memory_space=pltpu.SMEM)
    hb = pl.BlockSpec(memory_space=pl.ANY)
    block = (CHUNK, ROWS, STEPS, COLS)
    dma = pltpu.SemaphoreType.DMA
    out = jax.ShapeDtypeStruct((6, ROWS, STEPS, COLS), F32)
    scratch = [
        pltpu.VMEM((2, GROUPS, FB * SENS, CELLS), BF16),
        pltpu.VMEM((CHUNKS, 16) + block, BF16),
        pltpu.VMEM((GROUPS, 32 * CHUNK, CELLS), BF16),
        pltpu.VMEM((CHUNK, NT, CELLS), BF16),
        pltpu.VMEM((CHUNKS, 2, 8) + block, BF16),
        pltpu.VMEM((CHUNKS, 8) + block, BF16),
        pltpu.VMEM((CHUNKS, 4) + block, BF16),
        pltpu.VMEM((CHUNKS, 6) + block, BF16),
        pltpu.VMEM((CHUNKS, 3) + block, BF16),
        pltpu.VMEM((CHUNKS,) + block, BF16),
        pltpu.VMEM((JOBS, 8, GROUPS, 2 * CHUNK, COLS), F32),
        pltpu.VMEM((6, EXT, STEPS, COLS), F32),
        pltpu.VMEM((6, EXT, STEPS, COLS), F32),
        pltpu.VMEM((6, ROWS + 2, STEPS, COLS), F32),
        pltpu.VMEM((32, COLS), F32),
        pltpu.VMEM((32, COLS), F32),
        pltpu.VMEM((EXT, STEPS, COLS), F32),
        pltpu.VMEM((EXT, STEPS, COLS), F32),
        pltpu.VMEM((EXT, STEPS, COLS), F32),
        pltpu.VMEM((EXT, STEPS, COLS), F32),
        pltpu.VMEM((EXT, STEPS, COLS), F32),
        pltpu.VMEM((16, CELLS), BF16),
        pltpu.VMEM((8, COLS), F32),
        dma((22,)),
        dma((4,)),
        dma((4,)),
        dma((CHUNKS, 18)),
        dma((CHUNKS, 18)),
        dma((CHUNKS,)),
        dma((CHUNKS,)),
        dma((CHUNKS, 4)),
        dma((CHUNKS, 4)),
        dma((CHUNKS, 6)),
        dma((CHUNKS, 6)),
        dma((CHUNKS, 3)),
        dma((CHUNKS, 3)),
        dma((CHUNKS,)),
        dma((CHUNKS,)),
        dma((CHUNKS, 7)),
        dma((JOBS, 7)),
        dma((2, CHUNKS, 2)),
        dma((2, CHUNKS, 2)),
    ]
    sol, res = pl.pallas_call(
        kernel,
        out_shape=(out, out),
        in_specs=[hb, hb, vm, vm, sm, sm, vm, vm],
        out_specs=(vm, vm),
        scratch_shapes=scratch,
        compiler_params=pltpu.CompilerParams(
            collective_id=0, has_side_effects=True, vmem_limit_bytes=60 * 1024 * 1024
        ),
    )(
        rhs_t,
        maps,
        stiffness,
        reaction,
        noise_weight,
        sensor_cell,
        jnp.asarray(table, BF16),
        jnp.asarray(table.T, BF16),
    )
    return (jnp.transpose(sol, (2, 0, 1, 3)), jnp.transpose(res, (2, 0, 1, 3)))


def solution(mesh):
    placed = (
        P("sensors", None, "cells", None),
        P(None, None, "sensors", "cells"),
        P("cells", None),
        P("cells", None),
        P(),
        P(),
    )
    return jax.shard_map(
        shards,
        mesh=mesh,
        in_specs=placed,
        out_specs=(P("sensors", None, "cells", None), P("sensors", None, "cells", None)),
        check_vma=False,
    )
```

```python
import functools
import math

import jax
import jax.numpy as jnp
import numpy as np
from jax import lax
from jax.experimental import pallas as pl
from jax.experimental.pallas import tpu as pltpu
from jax.sharding import PartitionSpec as P

MESH = pl.DeviceIdType.MESH
BF16 = jnp.bfloat16
F32 = jnp.float32
DAMPING = 0.8
ROWS = 16
HALO = 4
EXT = ROWS + 2 * HALO
STEPS = 16
COLS = 128
CELLS = ROWS * COLS
NT = 256
FB = 16
GROUPS = 8
SENS = 8
CHUNK = 1
CHUNKS = 6 // CHUNK
SPLIT = 8
FIRST = pl.ds(0, SPLIT)
REST = pl.ds(SPLIT, ROWS - SPLIT)
PASS = 2
PASSES = 12 // PASS
ORDER = (
    ("update", 0, 0),
    ("a0", 0, 0),
    ("a2", 0, 1),
    ("idft", 1, 2),
    ("r1", 0, 2),
    ("a2", 1, 1),
    ("a3", 0, 1),
    ("dft", 0, 1),
    ("r1", 1, 2),
    ("a3", 1, 1),
    ("dft", 1, 1),
    ("oa", 0, 1),
    ("ob", 0, 1),
    ("r2", 0, 2),
    ("update", 1, 0),
    ("a0", 1, 0),
    ("r2", 1, 2),
    ("a1", 0, 0),
    ("r3", 0, 2),
    ("pa", 0, 1),
    ("pb", 0, 1),
    ("a1", 1, 0),
    ("idft", 0, 1),
    ("r3", 1, 2),
)
JOBS = 2 * CHUNKS


def transform_tables():
    wave = np.arange(128)[:, None]
    moment = np.arange(NT)[None, :]
    phase = (wave * moment % NT).astype(np.float32) * np.float32(2.0 * math.pi / NT)
    factor = np.float32(1.0 / math.sqrt(NT))
    real = (np.cos(phase) * factor).reshape(GROUPS, 1, FB, NT)
    imag = (-np.sin(phase) * factor).reshape(GROUPS, 1, FB, NT)
    return np.concatenate([real, imag], axis=1).reshape(NT, NT)


def kernel(
    rhs_hbm,
    map_hbm,
    stiff_ref,
    react_ref,
    weight_sm,
    cell_sm,
    table_ref,
    table_t_ref,
    sol_ref,
    res_ref,
    gv,
    xg,
    spec,
    adj,
    y,
    rsib,
    rzf,
    rxg,
    rxf,
    rzg,
    oall,
    rhs_ext,
    res_ext,
    hin,
    hout,
    stage,
    xf,
    sx,
    qx,
    sxin,
    c_sw,
    c_k,
    c_s,
    c_si,
    c_d,
    marks,
    nwt,
    loc_sem,
    init_sem,
    ag_send,
    ag_recv,
    rs_send,
    rs_recv,
    o_send,
    o_recv,
    halo_send,
    halo_recv,
):
    c_me = lax.axis_index("cells")
    s_me = lax.axis_index("sensors")
    core = lax.rem(s_me, 2)
    chip = s_me // 2
    xpos = lax.rem(chip, 4)
    zpos = chip // 4

    def sidx(dz, dx, cc):
        return (lax.rem(zpos + dz, 2) * 4 + lax.rem(xpos + dx, 4)) * 2 + cc

    other = 1 - core
    sib = {"sensors": sidx(0, 0, other)}
    xp = {"sensors": sidx(0, 1, core)}
    xm = {"sensors": sidx(0, 3, core)}
    zp = {"sensors": sidx(1, 0, core)}
    xd = {"sensors": sidx(0, 2, core)}
    xto = {1: xp, 2: xd, 3: xm}
    cnext = {"cells": lax.rem(c_me + 1, 8)}
    cprev = {"cells": lax.rem(c_me + 7, 8)}

    def rdma(src, dst, ss, rs, dev):
        return pltpu.make_async_remote_copy(
            src_ref=src, dst_ref=dst, send_sem=ss, recv_sem=rs, device_id=dev, device_id_type=MESH
        )

    def drain(ref, sem):
        pltpu.make_async_copy(ref, ref, sem).wait()

    map_copies = [
        pltpu.make_async_copy(map_hbm.at[p, g], gv.at[p, g], loc_sem.at[6])
        for p in range(2)
        for g in range(GROUPS)
    ]
    rhs_copies = [
        pltpu.make_async_copy(
            rhs_hbm.at[:, b], stage.at[b], loc_sem.at[b]
        )
        for b in range(6)
    ]
    for cp in rhs_copies:
        cp.start()
    for cp in map_copies:
        cp.start()

    barrier = pltpu.get_barrier_semaphore()
    peers = [sib, xp, xm, xd, zp] + [{"cells": lax.rem(c_me + j, 8)} for j in range(1, 8)]
    for peer in peers:
        pl.semaphore_signal(barrier, inc=1, device_id=peer, device_id_type=MESH)
    pl.semaphore_wait(barrier, len(peers))

    def coef_copies():
        return [
            rdma(stiff_ref.at[pl.ds(8, 8)], sxin.at[0], init_sem.at[0], init_sem.at[1], cnext),
            rdma(stiff_ref.at[pl.ds(0, 8)], sxin.at[1], init_sem.at[0], init_sem.at[1], cprev),
            rdma(react_ref.at[pl.ds(8, 8)], sxin.at[2], init_sem.at[0], init_sem.at[1], cnext),
            rdma(react_ref.at[pl.ds(0, 8)], sxin.at[3], init_sem.at[0], init_sem.at[1], cprev),
        ]

    def halo_start(ref, phase, k):
        for n, lo, dev in ((0, ROWS, cnext), (1, HALO, cprev)):
            hout[phase, k, n] = ref[k, pl.ds(lo, HALO)].astype(BF16)
            rdma(hout.at[phase, k, n], hin.at[phase, k, n], halo_send.at[phase, k], halo_recv.at[phase, k], dev).start()

    def halo_finish(ref, phase, k):
        drain(hin.at[phase, k], halo_recv.at[phase, k])
        drain(hout.at[phase, k], halo_send.at[phase, k])
        for n, lo in ((0, 0), (1, HALO + ROWS)):
            ref[k, pl.ds(lo, HALO)] = hin[phase, k, n].astype(F32)

    first = coef_copies()
    for cp in first:
        cp.start()
    for b in range(6):
        rhs_copies[b].wait()
        flat = stage.at[b].reshape(STEPS * ROWS, COLS)
        for r in range(ROWS):
            rhs_ext[b, HALO + r] = flat[pl.ds(r, STEPS, stride=ROWS), :]
        halo_start(rhs_ext, 0, b)

    lane = lax.broadcasted_iota(jnp.int32, (8, COLS), 1)
    acc = jnp.zeros((8, COLS), F32)
    for s in range(SENS):
        acc = jnp.where(lax.rem(lane, 8) == s, weight_sm[s_me * SENS + s], acc)
    nwt[...] = acc
    row = lax.broadcasted_iota(jnp.int32, (16, 512), 0)
    target = jnp.zeros((16, 512), jnp.int32)
    for s in range(SENS):
        target = jnp.where(lax.rem(row, 8) == s, cell_sm[s_me * SENS + s], target)
    for part in range(4):
        cell_id = lax.broadcasted_iota(jnp.int32, (16, 512), 1) + (c_me * CELLS + part * 512)
        marks[:, part * 512 : (part + 1) * 512] = jnp.where(cell_id == target, 1.0, 0.0).astype(BF16)

    sx[8:24, :] = stiff_ref[...]
    qx[8:24, :] = react_ref[...]
    drain(sxin, init_sem.at[0])
    drain(sxin, init_sem.at[1])
    sx[0:8, :] = sxin[0]
    sx[24:32, :] = sxin[1]
    qx[0:8, :] = sxin[2]
    qx[24:32, :] = sxin[3]
    erow = lax.broadcasted_iota(jnp.int32, (32, COLS), 0) + (c_me * ROWS - 8)
    inside = jnp.logical_and(erow >= 0, erow < 128)
    st = jnp.where(inside, sx[...], 0.0)
    re = jnp.where(inside, qx[...], 1.0)
    dg = re + 4.0 * st * st
    wv = DAMPING / dg
    si = jnp.where(inside, 1.0 / jnp.where(inside, st, 1.0), 0.0)
    for ref, val in ((c_sw, st * wv), (c_k, st * st * wv), (c_s, st), (c_si, si), (c_d, dg)):
        ref[...] = jnp.broadcast_to(val[8 - HALO : 8 - HALO + EXT][:, None, :], (EXT, STEPS, COLS))

    lane_s = lax.broadcasted_iota(jnp.int32, (STEPS, COLS), 1)
    not_first = lane_s > 0
    not_last = lane_s < COLS - 1

    def sides(v):
        left = pltpu.roll(v, 1, 1)
        right = pltpu.roll(v, COLS - 1, 1)
        return jnp.where(not_first, left, 0.0) + jnp.where(not_last, right, 0.0)

    def precondition(src, b, mode):
        levels = [{}, {}, {}]
        first = {}
        for r in range(EXT + 3):
            if r < EXT:
                first[r] = c_sw[r] * src[b, r]
                levels[0][r] = first[r]
            for n in range(3):
                q = r - 1 - n
                if not n + 1 <= q <= EXT - 2 - n:
                    continue
                now = levels[n]
                nb = now[q - 1] + now[q + 1] + sides(now[q])
                new = (1.0 - DAMPING) * now[q] + first[q] + c_k[q] * nb
                if n < 2:
                    levels[n + 1][q] = new
                elif mode == 0:
                    xf[b, q - 3] = c_si[q] * new
                elif mode == 1:
                    xf[b, q - 3] = xf[b, q - 3] + c_si[q] * new
                elif HALO <= q < HALO + ROWS:
                    sol_ref[b, q - HALO] = xf[b, q - 3] + c_si[q] * new

    d_me = s_me

    def ag_copy(k, idx, dz, dx, rows, dev):
        d = sidx(dz, dx, core)
        ref = xg.at[k, d] if rows is None else xg.at[k, d, :, rows]
        which = {1: 0, 2: 1, 3: 2, 4: 3}.get(idx, 4 if 5 <= idx <= 10 else 5)
        return rdma(ref, ref, ag_send.at[k], ag_recv.at[k, which], dev)

    def ag_copies(k):
        table = [
            (0, 0, None, sib),
            (0, 0, None, xp),
            (0, 0, None, xm),
            (0, 0, None, xd),
            (0, 0, None, zp),
            (1, 0, REST, xp),
            (1, 0, REST, xm),
            (1, 0, REST, xd),
            (0, 3, FIRST, zp),
            (0, 1, FIRST, zp),
            (0, 2, FIRST, zp),
            (0, 3, None, sib),
            (0, 1, None, sib),
            (0, 2, None, sib),
            (1, 0, None, sib),
            (1, 3, None, sib),
            (1, 1, None, sib),
            (1, 2, None, sib),
        ]
        return [ag_copy(k, i, *row) for i, row in enumerate(table)]

    def a0(u):
        k = lax.rem(u, CHUNKS)
        own_to_gather(k)
        s = ag_copies(k)
        for i in (4, 1, 2, 3, 0):
            s[i].start()

    def a1(u):
        s = ag_copies(lax.rem(u, CHUNKS))
        s[4].wait_recv()
        for i in (5, 6, 7, 14):
            s[i].start()
        for i, z, f in ((1, 8, 11), (2, 9, 12), (3, 10, 13)):
            s[i].wait_recv()
            s[z].start()
            s[f].start()

    def a2(u):
        k = lax.rem(u, CHUNKS)
        s = ag_copies(k)
        drain(xg.at[k, pl.ds(0, 3)], ag_recv.at[k, 4])
        for f in (15, 16, 17):
            s[f].start()

    def a3(u):
        k = lax.rem(u, CHUNKS)
        drain(xg.at[k, pl.ds(0, 8)], ag_recv.at[k, 5])
        drain(xg.at[k, pl.ds(0, 15)], ag_send.at[k])

    frow = lax.broadcasted_iota(jnp.int32, (FB, COLS), 0)
    fold = frow == lax.broadcasted_iota(jnp.int32, (FB, COLS), 1) // SENS

    def o_copies(w):
        n = lax.rem(w, 2)
        return [
            rdma(
                oall.at[w, c_me], oall.at[w, c_me], o_send.at[n], o_recv.at[w],
                {"cells": lax.rem(c_me + j, 8)},
            )
            for j in range(1, 8)
        ]

    def dft(u, sub):
        k = lax.rem(u, CHUNKS)
        for rp in range(ROWS // 2):
            x0 = xg[k, :, 0, 2 * rp].reshape(NT, COLS)
            x1 = xg[k, :, 0, 2 * rp + 1].reshape(NT, COLS)
            both = jnp.concatenate([x0, x1], axis=1)
            v = jnp.dot(table_ref[...], both, preferred_element_type=F32).astype(BF16)
            spec[:, sub * 32 : sub * 32 + 32, rp * 256 : rp * 256 + 256] = v.reshape(GROUPS, 32, 256)

    def observe(w, lo):
        for g in range(lo, lo + GROUPS // 2):
            vg = spec[g]
            parts = []
            for p in range(2):
                o = lax.dot_general(
                    vg, gv[p, g], (((1,), (1,)), ((), ())), preferred_element_type=F32
                ).reshape(2 * PASS, FB, COLS)
                parts.append(jnp.sum(jnp.where(fold[None], o, 0.0), axis=1))
            a, b = parts
            rows = []
            for n in range(PASS):
                rows.append(a[2 * n : 2 * n + 1] - b[2 * n + 1 : 2 * n + 2])
                rows.append(a[2 * n + 1 : 2 * n + 2] + b[2 * n : 2 * n + 1])
            oall[w, c_me, g] = jnp.concatenate(rows, axis=0)

    def oa(w):
        observe(w, 0)

    def ob(w):
        observe(w, GROUPS // 2)
        for cp in o_copies(w):
            cp.start()

    def sib_copy(k):
        return rdma(y.at[k, other], rsib.at[k], rs_send.at[k], rs_recv.at[k, 0], sib)

    def pull(w, lo):
        for g in range(lo, lo + GROUPS // 2):
            tot = oall[w, 0, g]
            for c in range(1, 8):
                tot = tot + oall[w, c, g]
            wt = nwt[0 : 2 * PASS] * tot
            rows = []
            for n in range(PASS):
                wr = jnp.broadcast_to(wt[2 * n : 2 * n + 1], (FB, COLS))
                wi = jnp.broadcast_to(wt[2 * n + 1 : 2 * n + 2], (FB, COLS))
                wr = jnp.where(fold, wr, 0.0)
                wi = jnp.where(fold, wi, 0.0)
                rows.append(jnp.concatenate([wr, wi], axis=1))
                rows.append(jnp.concatenate([wi, -wr], axis=1))
            wm = jnp.concatenate(rows, axis=0).astype(BF16)
            for part in range(4):
                cols = slice(part * 512, part * 512 + 512)
                gg = jnp.concatenate([gv[0, g, :, cols], gv[1, g, :, cols]], axis=0)
                a = jnp.dot(wm, gg, preferred_element_type=F32).astype(BF16)
                for n in range(PASS):
                    adj[n, g * 32 : g * 32 + 32, cols] = a[n * 32 : n * 32 + 32]

    def pa(w):
        drain(oall.at[w, pl.ds(0, 7)], o_recv.at[w])
        pull(w, 0)

    def pb(w):
        pull(w, GROUPS // 2)
        drain(oall.at[w, pl.ds(0, 7)], o_send.at[lax.rem(w, 2)])

    def idft(u, sub):
        k = lax.rem(u, CHUNKS)
        for rp in range(ROWS // 2):
            v = jnp.dot(
                table_t_ref[...], adj[sub, :, rp * 256 : rp * 256 + 256], preferred_element_type=F32
            ).astype(BF16)
            for half in range(2):
                part = v[:, half * COLS : half * COLS + COLS].reshape(8, 2, STEPS, COLS)
                for c in range(2):
                    y[k, c, :, 0, 2 * rp + half] = part[:, c]
        sib_copy(k).start()

    def block(zr, dx):
        return sidx(zr, dx, 0) // 2

    def total(k, zr, dx, bb, rs, arrived):
        ci = block(zr, dx)
        tot = y[k, core, ci, bb, rs].astype(F32) + rsib[k, ci, bb, rs].astype(F32)
        for ref in arrived:
            tot = tot + ref[bb, rs].astype(F32)
        return tot

    def add_rows(k, zr, dx, lo, hi, arrived):
        for bb in range(CHUNK):
            for r in range(lo, hi, 2):
                rs = pl.ds(r, 2)
                y[k, core, block(zr, dx), bb, rs] = total(k, zr, dx, bb, rs, arrived).astype(BF16)

    def rzf_copy(k, dx):
        return rdma(
            y.at[k, core, block(1, dx), :, FIRST], rzf.at[k, dx, :, FIRST], rs_send.at[k], rs_recv.at[k, dx or 5], zp
        )

    def rxg_copy(k, zr, dx):
        i = zr * 3 + dx - 1
        return rdma(
            y.at[k, core, block(zr, dx), :, REST], rxg.at[k, i, :, REST], rs_send.at[k], rs_recv.at[k, 5 - zr], xto[dx]
        )

    def rxf_copy(k, dx):
        i = dx - 1
        return rdma(
            y.at[k, core, block(0, dx), :, FIRST], rxf.at[k, i, :, FIRST], rs_send.at[k], rs_recv.at[k, 5], xto[dx]
        )

    def rzg_copy(k):
        return rdma(
            y.at[k, core, block(1, 0), :, REST], rzg.at[k, :, REST], rs_send.at[k], rs_recv.at[k, 5], zp
        )

    def r1(u):
        k = lax.rem(u, CHUNKS)
        sib_copy(k).wait_recv()
        for dx in (2, 1, 3):
            add_rows(k, 1, dx, 0, SPLIT, ())
            rzf_copy(k, dx).start()
            add_rows(k, 1, dx, SPLIT, ROWS, ())
            rxg_copy(k, 1, dx).start()
        add_rows(k, 1, 0, 0, SPLIT, ())
        rzf_copy(k, 0).start()
        for dx in (2, 1, 3):
            add_rows(k, 0, dx, SPLIT, ROWS, ())
            rxg_copy(k, 0, dx).start()

    def r2(u):
        k = lax.rem(u, CHUNKS)
        for dx in (2, 1, 3):
            rzf_copy(k, dx).wait_recv()
            add_rows(k, 0, dx, 0, SPLIT, (rzf.at[k, dx],))
            rxf_copy(k, dx).start()
        drain(rxg.at[k, pl.ds(3, 3), :, REST], rs_recv.at[k, 4])
        add_rows(k, 1, 0, SPLIT, ROWS, [rxg.at[k, 3 + i] for i in range(3)])
        rzg_copy(k).start()

    def r3(u):
        k = lax.rem(u, CHUNKS)
        drain(rxg.at[k, pl.ds(0, 4)], rs_recv.at[k, 5])
        for bb in range(CHUNK):
            b = k * CHUNK + bb
            for i in range(0, ROWS, 2):
                er = pl.ds(HALO + i, 2)
                rs = pl.ds(i, 2)
                us = [c_s[HALO + i - 1 + n] * xf[b, i + n] for n in range(4)]
                if i < SPLIT:
                    arrived = [rzf.at[k, 0]] + [rxf.at[k, n] for n in range(3)]
                else:
                    arrived = [rzg.at[k]] + [rxg.at[k, n] for n in range(3)]
                m = total(k, 0, 0, bb, rs, arrived)
                for n in range(2):
                    e = HALO + i + n
                    nb = us[n] + us[n + 2] + sides(us[n + 1])
                    prior = c_d[e] * xf[b, i + n + 1] - c_s[e] * nb
                    r = rhs_ext[b, e] - (prior + m[n])
                    res_ext[b, e] = r
                    res_ref[b, i + n] = r
        halo_start(res_ext, 1, k)
        drain(xg.at[k, pl.ds(0, 15)], rs_send.at[k])

    def own_to_gather(k):
        for bb in range(CHUNK):
            b = k * CHUNK + bb

            def body(i, carry, b=b, bb=bb):
                xg[k, d_me, bb, pl.ds(i * 4, 4)] = xf[b, pl.ds(1 + i * 4, 4)].astype(BF16)
                return carry

            lax.fori_loop(0, ROWS // 4, body, 0, unroll=4)

    def begin(k):
        halo_finish(rhs_ext, 0, k)
        for bb in range(CHUNK):
            b = k * CHUNK + bb
            precondition(rhs_ext, b, 0)

    def update(k, mode):
        halo_finish(res_ext, 1, k)

        for bb in range(CHUNK):
            precondition(res_ext, k * CHUNK + bb, mode)

    def finish_map():
        drain(gv, loc_sem.at[6])

        def body(i, carry):
            rs = pl.ds(pl.multiple_of(lax.rem(i, 8) * 16, 16), 16)
            g = i // 8
            gv[0, g, rs] = gv[0, g, rs] + marks[...]
            return carry

        lax.fori_loop(0, 64, body, 0, unroll=4)

    def advance(u):
        @pl.when(u < CHUNKS)
        def _():
            begin(u)

        @pl.when(jnp.logical_and(u >= CHUNKS, u < JOBS))
        def _():
            update(lax.rem(u, CHUNKS), 1)

        @pl.when(u >= JOBS)
        def _():
            update(lax.rem(u, CHUNKS), 2)

    stages = {"a0": a0, "a1": a1, "a2": a2, "a3": a3, "r1": r1, "r2": r2, "r3": r3}
    sampled = {"dft": dft, "idft": idft}
    passes = {"oa": oa, "ob": ob, "pa": pa, "pb": pb}

    def step(t, carry):
        for name, sub, late in ORDER:
            w = t - late

            def run(name=name, sub=sub, w=w):
                if name == "update":
                    advance(w * PASS + sub)
                elif name in stages:
                    stages[name](w * PASS + sub)
                elif name in sampled:
                    sampled[name](w * PASS + sub, sub)
                else:
                    passes[name](w)

            last = PASSES + PASSES // 2 if name == "update" else PASSES
            pl.when(jnp.logical_and(w >= 0, w < last))(run)
            if name == "a0" and sub == PASS - 1:
                pl.when(t == 0)(finish_map)
        return carry

    lax.fori_loop(0, PASSES + PASSES // 2, step, 0)


def shards(rhs, forward_map, stiffness, reaction, noise_weight, sensor_cell):
    table = transform_tables()
    maps = forward_map.reshape(2, GROUPS, FB * SENS, CELLS)
    vm = pl.BlockSpec(memory_space=pltpu.VMEM)
    sm = pl.BlockSpec(memory_space=pltpu.SMEM)
    hb = pl.BlockSpec(memory_space=pl.ANY)
    block = (CHUNK, ROWS, STEPS, COLS)
    dma = pltpu.SemaphoreType.DMA
    out = jax.ShapeDtypeStruct((6, ROWS, STEPS, COLS), F32)
    scratch = [
        pltpu.VMEM((2, GROUPS, FB * SENS, CELLS), BF16),
        pltpu.VMEM((CHUNKS, 16) + block, BF16),
        pltpu.VMEM((GROUPS, 32 * PASS, CELLS), BF16),
        pltpu.VMEM((PASS, NT, CELLS), BF16),
        pltpu.VMEM((CHUNKS, 2, 8) + block, BF16),
        pltpu.VMEM((CHUNKS, 8) + block, BF16),
        pltpu.VMEM((CHUNKS, 4) + block, BF16),
        pltpu.VMEM((CHUNKS, 6) + block, BF16),
        pltpu.VMEM((CHUNKS, 3) + block, BF16),
        pltpu.VMEM((CHUNKS,) + block, BF16),
        pltpu.VMEM((PASSES, 8, GROUPS, 2 * PASS, COLS), F32),
        pltpu.VMEM((6, EXT, STEPS, COLS), F32),
        pltpu.VMEM((6, EXT, STEPS, COLS), F32),
        pltpu.VMEM((2, CHUNKS, 2, HALO, STEPS, COLS), BF16),
        pltpu.VMEM((2, CHUNKS, 2, HALO, STEPS, COLS), BF16),
        pltpu.VMEM((6, STEPS, ROWS, COLS), F32),
        pltpu.VMEM((6, ROWS + 2, STEPS, COLS), F32),
        pltpu.VMEM((32, COLS), F32),
        pltpu.VMEM((32, COLS), F32),
        pltpu.VMEM((4, 8, COLS), F32),
        pltpu.VMEM((EXT, STEPS, COLS), F32),
        pltpu.VMEM((EXT, STEPS, COLS), F32),
        pltpu.VMEM((EXT, STEPS, COLS), F32),
        pltpu.VMEM((EXT, STEPS, COLS), F32),
        pltpu.VMEM((EXT, STEPS, COLS), F32),
        pltpu.VMEM((16, CELLS), BF16),
        pltpu.VMEM((8, COLS), F32),
        dma((7,)),
        dma((2,)),
        dma((CHUNKS,)),
        dma((CHUNKS, 6)),
        dma((CHUNKS,)),
        dma((CHUNKS, 6)),
        dma((2,)),
        dma((PASSES,)),
        dma((2, CHUNKS)),
        dma((2, CHUNKS)),
    ]
    sol, res = pl.pallas_call(
        kernel,
        out_shape=(out, out),
        in_specs=[hb, hb, vm, vm, sm, sm, vm, vm],
        out_specs=(vm, vm),
        scratch_shapes=scratch,
        compiler_params=pltpu.CompilerParams(
            collective_id=0, has_side_effects=True, vmem_limit_bytes=60 * 1024 * 1024
        ),
    )(
        rhs,
        maps,
        stiffness,
        reaction,
        noise_weight,
        sensor_cell,
        jnp.asarray(table, BF16),
        jnp.asarray(table.T, BF16),
    )
    return (jnp.transpose(sol, (2, 0, 1, 3)), jnp.transpose(res, (2, 0, 1, 3)))


def solution(mesh):
    placed = (
        P("sensors", None, "cells", None),
        P(None, None, "sensors", "cells"),
        P("cells", None),
        P("cells", None),
        P(),
        P(),
    )
    return jax.shard_map(
        shards,
        mesh=mesh,
        in_specs=placed,
        out_specs=(P("sensors", None, "cells", None), P("sensors", None, "cells", None)),
        check_vma=False,
    )
```

```python
import functools
import math

import jax
import jax.numpy as jnp
import numpy as np
from jax import lax
from jax.experimental import pallas as pl
from jax.experimental.pallas import tpu as pltpu
from jax.sharding import PartitionSpec as P

MESH = pl.DeviceIdType.MESH
BF16 = jnp.bfloat16
F32 = jnp.float32
DAMPING = 0.8
ROWS = 16
HALO = 4
EXT = ROWS + 2 * HALO
STEPS = 16
COLS = 128
CELLS = ROWS * COLS
NT = 256
FB = 16
GROUPS = 8
SENS = 8
CHUNK = 1
CHUNKS = 6 // CHUNK
SPLIT = 8
FIRST = pl.ds(0, SPLIT)
REST = pl.ds(SPLIT, ROWS - SPLIT)
PASS = 2
PASSES = 12 // PASS
ORDER = (
    ("update", 0, 0),
    ("a0", 0, 0),
    ("a2", 0, 1),
    ("idft", 1, 2),
    ("r1", 0, 2),
    ("a2", 1, 1),
    ("a3", 0, 1),
    ("dft", 0, 1),
    ("r1", 1, 2),
    ("a3", 1, 1),
    ("dft", 1, 1),
    ("oa", 0, 1),
    ("ob", 0, 1),
    ("r2", 0, 2),
    ("update", 1, 0),
    ("a0", 1, 0),
    ("r2", 1, 2),
    ("a1", 0, 0),
    ("r3", 0, 2),
    ("pa", 0, 1),
    ("pb", 0, 1),
    ("a1", 1, 0),
    ("idft", 0, 1),
    ("r3", 1, 2),
)
JOBS = 2 * CHUNKS


def transform_tables():
    wave = np.arange(128)[:, None]
    moment = np.arange(NT)[None, :]
    phase = (wave * moment % NT).astype(np.float32) * np.float32(2.0 * math.pi / NT)
    factor = np.float32(1.0 / math.sqrt(NT))
    real = (np.cos(phase) * factor).reshape(GROUPS, 1, FB, NT)
    imag = (-np.sin(phase) * factor).reshape(GROUPS, 1, FB, NT)
    return np.concatenate([real, imag], axis=1).reshape(NT, NT)


def kernel(
    rhs_hbm,
    map_hbm,
    stiff_ref,
    react_ref,
    weight_sm,
    cell_sm,
    table_ref,
    table_t_ref,
    sol_ref,
    res_ref,
    gv,
    xg,
    spec,
    adj,
    y,
    rsib,
    rzf,
    rxg,
    rxf,
    rzg,
    oall,
    rhs_ext,
    res_ext,
    hin,
    hout,
    stage,
    xf,
    sx,
    qx,
    sxin,
    c_sw,
    c_k,
    c_s,
    c_si,
    c_d,
    marks,
    nwt,
    loc_sem,
    init_sem,
    ag_send,
    ag_recv,
    rs_send,
    rs_recv,
    o_send,
    o_recv,
    halo_send,
    halo_recv,
):
    c_me = lax.axis_index("cells")
    s_me = lax.axis_index("sensors")
    core = lax.rem(s_me, 2)
    chip = s_me // 2
    xpos = lax.rem(chip, 4)
    zpos = chip // 4

    def sidx(dz, dx, cc):
        return (lax.rem(zpos + dz, 2) * 4 + lax.rem(xpos + dx, 4)) * 2 + cc

    other = 1 - core
    sib = {"sensors": sidx(0, 0, other)}
    xp = {"sensors": sidx(0, 1, core)}
    xm = {"sensors": sidx(0, 3, core)}
    zp = {"sensors": sidx(1, 0, core)}
    xd = {"sensors": sidx(0, 2, core)}
    xto = {1: xp, 2: xd, 3: xm}
    cnext = {"cells": lax.rem(c_me + 1, 8)}
    cprev = {"cells": lax.rem(c_me + 7, 8)}

    def rdma(src, dst, ss, rs, dev):
        return pltpu.make_async_remote_copy(
            src_ref=src, dst_ref=dst, send_sem=ss, recv_sem=rs, device_id=dev, device_id_type=MESH
        )

    def drain(ref, sem):
        pltpu.make_async_copy(ref, ref, sem).wait()

    map_copies = [
        pltpu.make_async_copy(map_hbm.at[p, g], gv.at[p, g], loc_sem.at[6])
        for p in range(2)
        for g in range(GROUPS)
    ]
    rhs_copies = [
        pltpu.make_async_copy(
            rhs_hbm.at[:, b], stage.at[b], loc_sem.at[b]
        )
        for b in range(6)
    ]
    for cp in rhs_copies:
        cp.start()
    for cp in map_copies:
        cp.start()

    barrier = pltpu.get_barrier_semaphore()
    peers = [sib, xp, xm, xd, zp] + [{"cells": lax.rem(c_me + j, 8)} for j in range(1, 8)]
    for peer in peers:
        pl.semaphore_signal(barrier, inc=1, device_id=peer, device_id_type=MESH)
    pl.semaphore_wait(barrier, len(peers))

    def coef_copies():
        return [
            rdma(stiff_ref.at[pl.ds(8, 8)], sxin.at[0], init_sem.at[0], init_sem.at[1], cnext),
            rdma(stiff_ref.at[pl.ds(0, 8)], sxin.at[1], init_sem.at[0], init_sem.at[1], cprev),
            rdma(react_ref.at[pl.ds(8, 8)], sxin.at[2], init_sem.at[0], init_sem.at[1], cnext),
            rdma(react_ref.at[pl.ds(0, 8)], sxin.at[3], init_sem.at[0], init_sem.at[1], cprev),
        ]

    def halo_start(ref, phase, k):
        for n, lo, dev in ((0, ROWS, cnext), (1, HALO, cprev)):
            hout[phase, k, n] = ref[k, pl.ds(lo, HALO)].astype(BF16)
            rdma(hout.at[phase, k, n], hin.at[phase, k, n], halo_send.at[phase, k], halo_recv.at[phase, k], dev).start()

    def halo_finish(ref, phase, k):
        drain(hin.at[phase, k], halo_recv.at[phase, k])
        drain(hout.at[phase, k], halo_send.at[phase, k])
        for n, lo in ((0, 0), (1, HALO + ROWS)):
            ref[k, pl.ds(lo, HALO)] = hin[phase, k, n].astype(F32)

    first = coef_copies()
    for cp in first:
        cp.start()
    for b in range(6):
        rhs_copies[b].wait()
        flat = stage.at[b].reshape(STEPS * ROWS, COLS)
        for r in range(ROWS):
            rhs_ext[b, HALO + r] = flat[pl.ds(r, STEPS, stride=ROWS), :]
        halo_start(rhs_ext, 0, b)

    lane = lax.broadcasted_iota(jnp.int32, (8, COLS), 1)
    acc = jnp.zeros((8, COLS), F32)
    for s in range(SENS):
        acc = jnp.where(lax.rem(lane, 8) == s, weight_sm[s_me * SENS + s], acc)
    nwt[...] = acc
    row = lax.broadcasted_iota(jnp.int32, (16, 512), 0)
    target = jnp.zeros((16, 512), jnp.int32)
    for s in range(SENS):
        target = jnp.where(lax.rem(row, 8) == s, cell_sm[s_me * SENS + s], target)
    for part in range(4):
        cell_id = lax.broadcasted_iota(jnp.int32, (16, 512), 1) + (c_me * CELLS + part * 512)
        marks[:, part * 512 : (part + 1) * 512] = jnp.where(cell_id == target, 1.0, 0.0).astype(BF16)

    sx[8:24, :] = stiff_ref[...]
    qx[8:24, :] = react_ref[...]
    drain(sxin, init_sem.at[0])
    drain(sxin, init_sem.at[1])
    sx[0:8, :] = sxin[0]
    sx[24:32, :] = sxin[1]
    qx[0:8, :] = sxin[2]
    qx[24:32, :] = sxin[3]
    erow = lax.broadcasted_iota(jnp.int32, (32, COLS), 0) + (c_me * ROWS - 8)
    inside = jnp.logical_and(erow >= 0, erow < 128)
    st = jnp.where(inside, sx[...], 0.0)
    re = jnp.where(inside, qx[...], 1.0)
    dg = re + 4.0 * st * st
    wv = DAMPING / dg
    si = jnp.where(inside, 1.0 / jnp.where(inside, st, 1.0), 0.0)
    for ref, val in ((c_sw, st * wv), (c_k, st * st * wv), (c_s, st), (c_si, si), (c_d, dg)):
        ref[...] = jnp.broadcast_to(val[8 - HALO : 8 - HALO + EXT][:, None, :], (EXT, STEPS, COLS))

    lane_s = lax.broadcasted_iota(jnp.int32, (STEPS, COLS), 1)
    not_first = lane_s > 0
    not_last = lane_s < COLS - 1

    def put_rows(ref, b, r, value):
        ref.reshape(STEPS * 6 * ROWS, COLS)[pl.ds(b * ROWS + r, STEPS, stride=6 * ROWS), :] = value

    def sides(v):
        left = pltpu.roll(v, 1, 1)
        right = pltpu.roll(v, COLS - 1, 1)
        return jnp.where(not_first, left, 0.0) + jnp.where(not_last, right, 0.0)

    def precondition(src, b, mode):
        levels = [{}, {}, {}]
        first = {}
        for r in range(EXT + 3):
            if r < EXT:
                first[r] = c_sw[r] * src[b, r]
                levels[0][r] = first[r]
            for n in range(3):
                q = r - 1 - n
                if not n + 1 <= q <= EXT - 2 - n:
                    continue
                now = levels[n]
                nb = now[q - 1] + now[q + 1] + sides(now[q])
                new = (1.0 - DAMPING) * now[q] + first[q] + c_k[q] * nb
                if n < 2:
                    levels[n + 1][q] = new
                elif mode == 0:
                    xf[b, q - 3] = c_si[q] * new
                elif mode == 1:
                    xf[b, q - 3] = xf[b, q - 3] + c_si[q] * new
                elif HALO <= q < HALO + ROWS:
                    put_rows(sol_ref, b, q - HALO, xf[b, q - 3] + c_si[q] * new)

    d_me = s_me

    def ag_copy(k, idx, dz, dx, rows, dev):
        d = sidx(dz, dx, core)
        ref = xg.at[k, d] if rows is None else xg.at[k, d, :, rows]
        which = {1: 0, 2: 1, 3: 2, 4: 3}.get(idx, 4 if 5 <= idx <= 10 else 5)
        return rdma(ref, ref, ag_send.at[k], ag_recv.at[k, which], dev)

    def ag_copies(k):
        table = [
            (0, 0, None, sib),
            (0, 0, None, xp),
            (0, 0, None, xm),
            (0, 0, None, xd),
            (0, 0, None, zp),
            (1, 0, REST, xp),
            (1, 0, REST, xm),
            (1, 0, REST, xd),
            (0, 3, FIRST, zp),
            (0, 1, FIRST, zp),
            (0, 2, FIRST, zp),
            (0, 3, None, sib),
            (0, 1, None, sib),
            (0, 2, None, sib),
            (1, 0, None, sib),
            (1, 3, None, sib),
            (1, 1, None, sib),
            (1, 2, None, sib),
        ]
        return [ag_copy(k, i, *row) for i, row in enumerate(table)]

    def a0(u):
        k = lax.rem(u, CHUNKS)
        own_to_gather(k)
        s = ag_copies(k)
        for i in (4, 1, 2, 3, 0):
            s[i].start()

    def a1(u):
        s = ag_copies(lax.rem(u, CHUNKS))
        s[4].wait_recv()
        for i in (5, 6, 7, 14):
            s[i].start()
        for i, z, f in ((1, 8, 11), (2, 9, 12), (3, 10, 13)):
            s[i].wait_recv()
            s[z].start()
            s[f].start()

    def a2(u):
        k = lax.rem(u, CHUNKS)
        s = ag_copies(k)
        drain(xg.at[k, pl.ds(0, 3)], ag_recv.at[k, 4])
        for f in (15, 16, 17):
            s[f].start()

    def a3(u):
        k = lax.rem(u, CHUNKS)
        drain(xg.at[k, pl.ds(0, 8)], ag_recv.at[k, 5])
        drain(xg.at[k, pl.ds(0, 15)], ag_send.at[k])

    frow = lax.broadcasted_iota(jnp.int32, (FB, COLS), 0)
    fold = frow == lax.broadcasted_iota(jnp.int32, (FB, COLS), 1) // SENS

    def o_copies(w):
        n = lax.rem(w, 2)
        return [
            rdma(
                oall.at[w, c_me], oall.at[w, c_me], o_send.at[n], o_recv.at[w],
                {"cells": lax.rem(c_me + j, 8)},
            )
            for j in range(1, 8)
        ]

    def dft(u, sub):
        k = lax.rem(u, CHUNKS)
        for rp in range(ROWS // 2):
            x0 = xg[k, :, 0, 2 * rp].reshape(NT, COLS)
            x1 = xg[k, :, 0, 2 * rp + 1].reshape(NT, COLS)
            both = jnp.concatenate([x0, x1], axis=1)
            v = jnp.dot(table_ref[...], both, preferred_element_type=F32).astype(BF16)
            spec[:, sub * 32 : sub * 32 + 32, rp * 256 : rp * 256 + 256] = v.reshape(GROUPS, 32, 256)

    def observe(w, lo):
        for g in range(lo, lo + GROUPS // 2):
            vg = spec[g]
            both = jnp.concatenate([gv[0, g], gv[1, g]], axis=0)
            o = lax.dot_general(vg, both, (((1,), (1,)), ((), ())), preferred_element_type=F32)
            parts = []
            for p in range(2):
                op = o[:, p * COLS : p * COLS + COLS].reshape(2 * PASS, FB, COLS)
                parts.append(jnp.sum(jnp.where(fold[None], op, 0.0), axis=1))
            a, b = parts
            rows = []
            for n in range(PASS):
                rows.append(a[2 * n : 2 * n + 1] - b[2 * n + 1 : 2 * n + 2])
                rows.append(a[2 * n + 1 : 2 * n + 2] + b[2 * n : 2 * n + 1])
            oall[w, c_me, g] = jnp.concatenate(rows, axis=0)

    def oa(w):
        observe(w, 0)

    def ob(w):
        observe(w, GROUPS // 2)
        for cp in o_copies(w):
            cp.start()

    def sib_copy(k):
        return rdma(y.at[k, other], rsib.at[k], rs_send.at[k], rs_recv.at[k, 0], sib)

    def pull(w, lo):
        for g in range(lo, lo + GROUPS // 2):
            tot = oall[w, 0, g]
            for c in range(1, 8):
                tot = tot + oall[w, c, g]
            wt = nwt[0 : 2 * PASS] * tot
            rows = []
            for n in range(PASS):
                wr = jnp.broadcast_to(wt[2 * n : 2 * n + 1], (FB, COLS))
                wi = jnp.broadcast_to(wt[2 * n + 1 : 2 * n + 2], (FB, COLS))
                wr = jnp.where(fold, wr, 0.0)
                wi = jnp.where(fold, wi, 0.0)
                rows.append(jnp.concatenate([wr, wi], axis=1))
                rows.append(jnp.concatenate([wi, -wr], axis=1))
            wm = jnp.concatenate(rows, axis=0).astype(BF16)
            for part in range(4):
                cols = slice(part * 512, part * 512 + 512)
                gg = jnp.concatenate([gv[0, g, :, cols], gv[1, g, :, cols]], axis=0)
                a = jnp.dot(wm, gg, preferred_element_type=F32).astype(BF16)
                for n in range(PASS):
                    adj[n, g * 32 : g * 32 + 32, cols] = a[n * 32 : n * 32 + 32]

    def pa(w):
        drain(oall.at[w, pl.ds(0, 7)], o_recv.at[w])
        pull(w, 0)

    def pb(w):
        pull(w, GROUPS // 2)
        drain(oall.at[w, pl.ds(0, 7)], o_send.at[lax.rem(w, 2)])

    def idft(u, sub):
        k = lax.rem(u, CHUNKS)
        for rp in range(ROWS // 2):
            v = jnp.dot(
                table_t_ref[...], adj[sub, :, rp * 256 : rp * 256 + 256], preferred_element_type=F32
            ).astype(BF16)
            for half in range(2):
                part = v[:, half * COLS : half * COLS + COLS].reshape(8, 2, STEPS, COLS)
                for c in range(2):
                    y[k, c, :, 0, 2 * rp + half] = part[:, c]
        sib_copy(k).start()

    def block(zr, dx):
        return sidx(zr, dx, 0) // 2

    def total(k, zr, dx, bb, rs, arrived):
        ci = block(zr, dx)
        tot = y[k, core, ci, bb, rs].astype(F32) + rsib[k, ci, bb, rs].astype(F32)
        for ref in arrived:
            tot = tot + ref[bb, rs].astype(F32)
        return tot

    def add_rows(k, zr, dx, lo, hi, arrived):
        for bb in range(CHUNK):
            for r in range(lo, hi, 2):
                rs = pl.ds(r, 2)
                y[k, core, block(zr, dx), bb, rs] = total(k, zr, dx, bb, rs, arrived).astype(BF16)

    def rzf_copy(k, dx):
        return rdma(
            y.at[k, core, block(1, dx), :, FIRST], rzf.at[k, dx, :, FIRST], rs_send.at[k], rs_recv.at[k, dx or 5], zp
        )

    def rxg_copy(k, zr, dx):
        i = zr * 3 + dx - 1
        return rdma(
            y.at[k, core, block(zr, dx), :, REST], rxg.at[k, i, :, REST], rs_send.at[k], rs_recv.at[k, 5 - zr], xto[dx]
        )

    def rxf_copy(k, dx):
        i = dx - 1
        return rdma(
            y.at[k, core, block(0, dx), :, FIRST], rxf.at[k, i, :, FIRST], rs_send.at[k], rs_recv.at[k, 5], xto[dx]
        )

    def rzg_copy(k):
        return rdma(
            y.at[k, core, block(1, 0), :, REST], rzg.at[k, :, REST], rs_send.at[k], rs_recv.at[k, 5], zp
        )

    def r1(u):
        k = lax.rem(u, CHUNKS)
        sib_copy(k).wait_recv()
        for dx in (2, 1, 3):
            add_rows(k, 1, dx, 0, SPLIT, ())
            rzf_copy(k, dx).start()
            add_rows(k, 1, dx, SPLIT, ROWS, ())
            rxg_copy(k, 1, dx).start()
        add_rows(k, 1, 0, 0, SPLIT, ())
        rzf_copy(k, 0).start()
        for dx in (2, 1, 3):
            add_rows(k, 0, dx, SPLIT, ROWS, ())
            rxg_copy(k, 0, dx).start()

    def r2(u):
        k = lax.rem(u, CHUNKS)
        for dx in (2, 1, 3):
            rzf_copy(k, dx).wait_recv()
            add_rows(k, 0, dx, 0, SPLIT, (rzf.at[k, dx],))
            rxf_copy(k, dx).start()
        drain(rxg.at[k, pl.ds(3, 3), :, REST], rs_recv.at[k, 4])
        add_rows(k, 1, 0, SPLIT, ROWS, [rxg.at[k, 3 + i] for i in range(3)])
        rzg_copy(k).start()

    def r3(u):
        k = lax.rem(u, CHUNKS)
        drain(rxg.at[k, pl.ds(0, 4)], rs_recv.at[k, 5])
        for bb in range(CHUNK):
            b = k * CHUNK + bb
            for i in range(0, ROWS, 2):
                er = pl.ds(HALO + i, 2)
                rs = pl.ds(i, 2)
                us = [c_s[HALO + i - 1 + n] * xf[b, i + n] for n in range(4)]
                if i < SPLIT:
                    arrived = [rzf.at[k, 0]] + [rxf.at[k, n] for n in range(3)]
                else:
                    arrived = [rzg.at[k]] + [rxg.at[k, n] for n in range(3)]
                m = total(k, 0, 0, bb, rs, arrived)
                for n in range(2):
                    e = HALO + i + n
                    nb = us[n] + us[n + 2] + sides(us[n + 1])
                    prior = c_d[e] * xf[b, i + n + 1] - c_s[e] * nb
                    r = rhs_ext[b, e] - (prior + m[n])
                    res_ext[b, e] = r
                    put_rows(res_ref, b, i + n, r)
        halo_start(res_ext, 1, k)
        drain(xg.at[k, pl.ds(0, 15)], rs_send.at[k])

    def own_to_gather(k):
        for bb in range(CHUNK):
            b = k * CHUNK + bb

            def body(i, carry, b=b, bb=bb):
                xg[k, d_me, bb, pl.ds(i * 4, 4)] = xf[b, pl.ds(1 + i * 4, 4)].astype(BF16)
                return carry

            lax.fori_loop(0, ROWS // 4, body, 0, unroll=4)

    def begin(k):
        halo_finish(rhs_ext, 0, k)
        for bb in range(CHUNK):
            b = k * CHUNK + bb
            precondition(rhs_ext, b, 0)

    def update(k, mode):
        halo_finish(res_ext, 1, k)

        for bb in range(CHUNK):
            precondition(res_ext, k * CHUNK + bb, mode)

    def finish_map():
        drain(gv, loc_sem.at[6])

        def body(i, carry):
            rs = pl.ds(pl.multiple_of(lax.rem(i, 8) * 16, 16), 16)
            g = i // 8
            gv[0, g, rs] = gv[0, g, rs] + marks[...]
            return carry

        lax.fori_loop(0, 64, body, 0, unroll=4)

    def advance(u):
        @pl.when(u < CHUNKS)
        def _():
            begin(u)

        @pl.when(jnp.logical_and(u >= CHUNKS, u < JOBS))
        def _():
            update(lax.rem(u, CHUNKS), 1)

        @pl.when(u >= JOBS)
        def _():
            update(lax.rem(u, CHUNKS), 2)

    stages = {"a0": a0, "a1": a1, "a2": a2, "a3": a3, "r1": r1, "r2": r2, "r3": r3}
    sampled = {"dft": dft, "idft": idft}
    passes = {"oa": oa, "ob": ob, "pa": pa, "pb": pb}

    def step(t, carry):
        for name, sub, late in ORDER:
            w = t - late

            def run(name=name, sub=sub, w=w):
                if name == "update":
                    advance(w * PASS + sub)
                elif name in stages:
                    stages[name](w * PASS + sub)
                elif name in sampled:
                    sampled[name](w * PASS + sub, sub)
                else:
                    passes[name](w)

            last = PASSES + PASSES // 2 if name == "update" else PASSES
            pl.when(jnp.logical_and(w >= 0, w < last))(run)
            if name == "a0" and sub == PASS - 1:
                pl.when(t == 0)(finish_map)
        return carry

    lax.fori_loop(0, PASSES + PASSES // 2, step, 0)


def write_out(a_ref, b_ref, a_out, b_out, sem):
    copies = [
        pltpu.make_async_copy(a_ref, a_out, sem.at[0]),
        pltpu.make_async_copy(b_ref, b_out, sem.at[1]),
    ]
    for cp in copies:
        cp.start()
    for cp in copies:
        cp.wait()


def shards(rhs, forward_map, stiffness, reaction, noise_weight, sensor_cell):
    table = transform_tables()
    maps = forward_map.reshape(2, GROUPS, FB * SENS, CELLS)
    vm = pl.BlockSpec(memory_space=pltpu.VMEM)
    sm = pl.BlockSpec(memory_space=pltpu.SMEM)
    hb = pl.BlockSpec(memory_space=pl.ANY)
    block = (CHUNK, ROWS, STEPS, COLS)
    dma = pltpu.SemaphoreType.DMA
    out = jax.ShapeDtypeStruct((STEPS, 6, ROWS, COLS), F32)
    scratch = [
        pltpu.VMEM((2, GROUPS, FB * SENS, CELLS), BF16),
        pltpu.VMEM((CHUNKS, 16) + block, BF16),
        pltpu.VMEM((GROUPS, 32 * PASS, CELLS), BF16),
        pltpu.VMEM((PASS, NT, CELLS), BF16),
        pltpu.VMEM((CHUNKS, 2, 8) + block, BF16),
        pltpu.VMEM((CHUNKS, 8) + block, BF16),
        pltpu.VMEM((CHUNKS, 4) + block, BF16),
        pltpu.VMEM((CHUNKS, 6) + block, BF16),
        pltpu.VMEM((CHUNKS, 3) + block, BF16),
        pltpu.VMEM((CHUNKS,) + block, BF16),
        pltpu.VMEM((PASSES, 8, GROUPS, 2 * PASS, COLS), F32),
        pltpu.VMEM((6, EXT, STEPS, COLS), F32),
        pltpu.VMEM((6, EXT, STEPS, COLS), F32),
        pltpu.VMEM((2, CHUNKS, 2, HALO, STEPS, COLS), BF16),
        pltpu.VMEM((2, CHUNKS, 2, HALO, STEPS, COLS), BF16),
        pltpu.VMEM((6, STEPS, ROWS, COLS), F32),
        pltpu.VMEM((6, ROWS + 2, STEPS, COLS), F32),
        pltpu.VMEM((32, COLS), F32),
        pltpu.VMEM((32, COLS), F32),
        pltpu.VMEM((4, 8, COLS), F32),
        pltpu.VMEM((EXT, STEPS, COLS), F32),
        pltpu.VMEM((EXT, STEPS, COLS), F32),
        pltpu.VMEM((EXT, STEPS, COLS), F32),
        pltpu.VMEM((EXT, STEPS, COLS), F32),
        pltpu.VMEM((EXT, STEPS, COLS), F32),
        pltpu.VMEM((16, CELLS), BF16),
        pltpu.VMEM((8, COLS), F32),
        dma((7,)),
        dma((2,)),
        dma((CHUNKS,)),
        dma((CHUNKS, 6)),
        dma((CHUNKS,)),
        dma((CHUNKS, 6)),
        dma((2,)),
        dma((PASSES,)),
        dma((2, CHUNKS)),
        dma((2, CHUNKS)),
    ]
    sol, res = pl.pallas_call(
        kernel,
        out_shape=(out, out),
        in_specs=[hb, hb, vm, vm, sm, sm, vm, vm],
        out_specs=(vm, vm),
        scratch_shapes=scratch,
        compiler_params=pltpu.CompilerParams(
            collective_id=0, has_side_effects=True, vmem_limit_bytes=60 * 1024 * 1024
        ),
    )(
        rhs,
        maps,
        stiffness,
        reaction,
        noise_weight,
        sensor_cell,
        jnp.asarray(table, BF16),
        jnp.asarray(table.T, BF16),
    )
    place = pl.BlockSpec(memory_space=pl.ANY)
    return pl.pallas_call(
        write_out,
        out_shape=(out, out),
        in_specs=[vm, vm],
        out_specs=(place, place),
        scratch_shapes=[dma((2,))],
    )(sol, res)


def solution(mesh):
    placed = (
        P("sensors", None, "cells", None),
        P(None, None, "sensors", "cells"),
        P("cells", None),
        P("cells", None),
        P(),
        P(),
    )
    return jax.shard_map(
        shards,
        mesh=mesh,
        in_specs=placed,
        out_specs=(P("sensors", None, "cells", None), P("sensors", None, "cells", None)),
        check_vma=False,
    )
```

```python
import functools
import math

import jax
import jax.numpy as jnp
import numpy as np
from jax import lax
from jax.experimental import pallas as pl
from jax.experimental.pallas import tpu as pltpu
from jax.sharding import PartitionSpec as P

MESH = pl.DeviceIdType.MESH
BF16 = jnp.bfloat16
F32 = jnp.float32
DAMPING = 0.8
ROWS = 16
HALO = 4
EXT = ROWS + 2 * HALO
STEPS = 16
COLS = 128
CELLS = ROWS * COLS
NT = 256
FB = 16
GROUPS = 8
SENS = 8
CHUNK = 1
CHUNKS = 6 // CHUNK
SPLIT = 8
FIRST = pl.ds(0, SPLIT)
REST = pl.ds(SPLIT, ROWS - SPLIT)
LOW = pl.ds(SPLIT, 4)
HIGH = pl.ds(SPLIT + 4, 4)
PASS = 2
PASSES = 12 // PASS
ORDER = (
    ("update", 0, 0),
    ("a0", 0, 0),
    ("a2", 0, 1),
    ("idft", 1, 2),
    ("r1", 0, 2),
    ("a3", 0, 1),
    ("a2", 1, 1),
    ("dft", 0, 1),
    ("r1", 1, 2),
    ("a3", 1, 1),
    ("dft", 1, 1),
    ("oa", 0, 1),
    ("ob", 0, 1),
    ("r2", 0, 2),
    ("update", 1, 0),
    ("a0", 1, 0),
    ("r2", 1, 2),
    ("a1", 0, 0),
    ("r3", 0, 2),
    ("pa", 0, 1),
    ("pb", 0, 1),
    ("a1", 1, 0),
    ("idft", 0, 1),
    ("r3", 1, 2),
)
JOBS = 2 * CHUNKS


def transform_tables():
    wave = np.arange(128)[:, None]
    moment = np.arange(NT)[None, :]
    phase = (wave * moment % NT).astype(np.float32) * np.float32(2.0 * math.pi / NT)
    factor = np.float32(1.0 / math.sqrt(NT))
    real = (np.cos(phase) * factor).reshape(GROUPS, 1, FB, NT)
    imag = (-np.sin(phase) * factor).reshape(GROUPS, 1, FB, NT)
    return np.concatenate([real, imag], axis=1).reshape(NT, NT)


def kernel(
    rhs_hbm,
    map_hbm,
    stiff_ref,
    react_ref,
    weight_sm,
    cell_sm,
    table_ref,
    table_t_ref,
    sol_out,
    res_out,
    gv,
    xg,
    spec,
    adj,
    y,
    rsib,
    rzf,
    rxg,
    rxf,
    rel,
    rzg,
    oall,
    rhs_ext,
    res_ext,
    hin,
    hout,
    stage,
    xf,
    sx,
    qx,
    sxin,
    c_sw,
    c_k,
    c_s,
    c_si,
    c_d,
    marks,
    nwt,
    sol_ref,
    res_ref,
    out_sem,
    loc_sem,
    init_sem,
    ag_send,
    ag_recv,
    rs_send,
    rs_recv,
    o_send,
    o_recv,
    halo_send,
    halo_recv,
):
    c_me = lax.axis_index("cells")
    s_me = lax.axis_index("sensors")
    core = lax.rem(s_me, 2)
    chip = s_me // 2
    xpos = lax.rem(chip, 4)
    zpos = chip // 4

    def sidx(dz, dx, cc):
        return (lax.rem(zpos + dz, 2) * 4 + lax.rem(xpos + dx, 4)) * 2 + cc

    other = 1 - core
    sib = {"sensors": sidx(0, 0, other)}
    xp = {"sensors": sidx(0, 1, core)}
    xm = {"sensors": sidx(0, 3, core)}
    zp = {"sensors": sidx(1, 0, core)}
    xd = {"sensors": sidx(0, 2, core)}
    xto = {1: xp, 2: xd, 3: xm}
    cnext = {"cells": lax.rem(c_me + 1, 8)}
    cprev = {"cells": lax.rem(c_me + 7, 8)}

    def rdma(src, dst, ss, rs, dev):
        return pltpu.make_async_remote_copy(
            src_ref=src, dst_ref=dst, send_sem=ss, recv_sem=rs, device_id=dev, device_id_type=MESH
        )

    def drain(ref, sem):
        pltpu.make_async_copy(ref, ref, sem).wait()

    map_copies = [
        pltpu.make_async_copy(map_hbm.at[p, g], gv.at[p, g], loc_sem.at[6])
        for p in range(2)
        for g in range(GROUPS)
    ]
    rhs_copies = [
        pltpu.make_async_copy(
            rhs_hbm.at[:, b], stage.at[b], loc_sem.at[b]
        )
        for b in range(6)
    ]
    for cp in rhs_copies:
        cp.start()
    for cp in map_copies:
        cp.start()

    barrier = pltpu.get_barrier_semaphore()
    peers = [sib, xp, xm, xd, zp] + [{"cells": lax.rem(c_me + j, 8)} for j in range(1, 8)]
    for peer in peers:
        pl.semaphore_signal(barrier, inc=1, device_id=peer, device_id_type=MESH)
    pl.semaphore_wait(barrier, len(peers))

    def coef_copies():
        return [
            rdma(stiff_ref.at[pl.ds(8, 8)], sxin.at[0], init_sem.at[0], init_sem.at[1], cnext),
            rdma(stiff_ref.at[pl.ds(0, 8)], sxin.at[1], init_sem.at[0], init_sem.at[1], cprev),
            rdma(react_ref.at[pl.ds(8, 8)], sxin.at[2], init_sem.at[0], init_sem.at[1], cnext),
            rdma(react_ref.at[pl.ds(0, 8)], sxin.at[3], init_sem.at[0], init_sem.at[1], cprev),
        ]

    def halo_start(ref, phase, k):
        for n, lo, dev in ((0, ROWS, cnext), (1, HALO, cprev)):
            hout[phase, k, n] = ref[k, pl.ds(lo, HALO)].astype(BF16)
            rdma(hout.at[phase, k, n], hin.at[phase, k, n], halo_send.at[phase, k], halo_recv.at[phase, k], dev).start()

    def halo_finish(ref, phase, k):
        drain(hin.at[phase, k], halo_recv.at[phase, k])
        drain(hout.at[phase, k], halo_send.at[phase, k])
        for n, lo in ((0, 0), (1, HALO + ROWS)):
            ref[k, pl.ds(lo, HALO)] = hin[phase, k, n].astype(F32)

    first = coef_copies()
    for cp in first:
        cp.start()
    for b in range(6):
        rhs_copies[b].wait()
        flat = stage.at[b].reshape(STEPS * ROWS, COLS)
        for r in range(ROWS):
            rhs_ext[b, HALO + r] = flat[pl.ds(r, STEPS, stride=ROWS), :]
        halo_start(rhs_ext, 0, b)

    lane = lax.broadcasted_iota(jnp.int32, (8, COLS), 1)
    acc = jnp.zeros((8, COLS), F32)
    for s in range(SENS):
        acc = jnp.where(lax.rem(lane, 8) == s, weight_sm[s_me * SENS + s], acc)
    nwt[...] = acc
    row = lax.broadcasted_iota(jnp.int32, (16, 512), 0)
    target = jnp.zeros((16, 512), jnp.int32)
    for s in range(SENS):
        target = jnp.where(lax.rem(row, 8) == s, cell_sm[s_me * SENS + s], target)
    for part in range(4):
        cell_id = lax.broadcasted_iota(jnp.int32, (16, 512), 1) + (c_me * CELLS + part * 512)
        marks[:, part * 512 : (part + 1) * 512] = jnp.where(cell_id == target, 1.0, 0.0).astype(BF16)

    sx[8:24, :] = stiff_ref[...]
    qx[8:24, :] = react_ref[...]
    drain(sxin, init_sem.at[0])
    drain(sxin, init_sem.at[1])
    sx[0:8, :] = sxin[0]
    sx[24:32, :] = sxin[1]
    qx[0:8, :] = sxin[2]
    qx[24:32, :] = sxin[3]
    erow = lax.broadcasted_iota(jnp.int32, (32, COLS), 0) + (c_me * ROWS - 8)
    inside = jnp.logical_and(erow >= 0, erow < 128)
    st = jnp.where(inside, sx[...], 0.0)
    re = jnp.where(inside, qx[...], 1.0)
    dg = re + 4.0 * st * st
    wv = DAMPING / dg
    si = jnp.where(inside, 1.0 / jnp.where(inside, st, 1.0), 0.0)
    for ref, val in ((c_sw, st * wv), (c_k, st * st * wv), (c_s, st), (c_si, si), (c_d, dg)):
        ref[...] = jnp.broadcast_to(val[8 - HALO : 8 - HALO + EXT][:, None, :], (EXT, STEPS, COLS))

    lane_s = lax.broadcasted_iota(jnp.int32, (STEPS, COLS), 1)
    not_first = lane_s > 0
    not_last = lane_s < COLS - 1

    def put_rows(ref, b, r, value):
        ref.reshape(STEPS * 6 * ROWS, COLS)[pl.ds(b * ROWS + r, STEPS, stride=6 * ROWS), :] = value

    def sides(v):
        left = pltpu.roll(v, 1, 1)
        right = pltpu.roll(v, COLS - 1, 1)
        return jnp.where(not_first, left, 0.0) + jnp.where(not_last, right, 0.0)

    def precondition(src, b, mode):
        levels = [{}, {}, {}]
        first = {}
        for r in range(EXT + 3):
            if r < EXT:
                first[r] = c_sw[r] * src[b, r]
                levels[0][r] = first[r]
            for n in range(3):
                q = r - 1 - n
                if not n + 1 <= q <= EXT - 2 - n:
                    continue
                now = levels[n]
                nb = now[q - 1] + now[q + 1] + sides(now[q])
                new = (1.0 - DAMPING) * now[q] + first[q] + c_k[q] * nb
                if n < 2:
                    levels[n + 1][q] = new
                elif mode == 0:
                    xf[b, q - 3] = c_si[q] * new
                elif mode == 1:
                    xf[b, q - 3] = xf[b, q - 3] + c_si[q] * new
                elif HALO <= q < HALO + ROWS:
                    put_rows(sol_ref, b, q - HALO, xf[b, q - 3] + c_si[q] * new)

    d_me = s_me

    def ag_copy(k, idx, dz, dx, rows, dev):
        d = sidx(dz, dx, core)
        ref = xg.at[k, d] if rows is None else xg.at[k, d, :, rows]
        which = {1: 0, 2: 1, 3: 2, 4: 3, 18: 6, 19: 6}.get(idx, 4 if 5 <= idx <= 10 else 5)
        return rdma(ref, ref, ag_send.at[k], ag_recv.at[k, which], dev)

    def ag_copies(k):
        table = [
            (0, 0, None, sib),
            (0, 0, None, xp),
            (0, 0, None, xm),
            (0, 0, FIRST, xd),
            (0, 0, None, zp),
            (1, 0, REST, xp),
            (1, 0, REST, xm),
            (1, 0, REST, xd),
            (0, 3, FIRST, zp),
            (0, 1, FIRST, zp),
            (0, 2, FIRST, zp),
            (0, 3, None, sib),
            (0, 1, None, sib),
            (0, 2, None, sib),
            (1, 0, None, sib),
            (1, 3, None, sib),
            (1, 1, None, sib),
            (1, 2, None, sib),
            (0, 3, LOW, xp),
            (0, 1, HIGH, xm),
        ]
        return [ag_copy(k, i, *row) for i, row in enumerate(table)]

    def a0(u):
        k = lax.rem(u, CHUNKS)
        own_to_gather(k)
        s = ag_copies(k)
        for i in (4, 1, 2, 3, 0):
            s[i].start()

    def a1(u):
        s = ag_copies(lax.rem(u, CHUNKS))
        s[4].wait_recv()
        for i in (5, 6, 7, 14):
            s[i].start()
        for i, more in ((1, (18, 8, 11)), (2, (19, 9, 12)), (3, (10,))):
            s[i].wait_recv()
            for n in more:
                s[n].start()

    def a2(u):
        k = lax.rem(u, CHUNKS)
        s = ag_copies(k)
        drain(xg.at[k, 0, :, REST], ag_recv.at[k, 6])
        s[13].start()
        drain(xg.at[k, pl.ds(0, 3)], ag_recv.at[k, 4])
        for f in (15, 16, 17):
            s[f].start()

    def a3(u):
        k = lax.rem(u, CHUNKS)
        drain(xg.at[k, pl.ds(0, 8)], ag_recv.at[k, 5])
        drain(xg.at[k, pl.ds(0, 15)], ag_send.at[k])

    frow = lax.broadcasted_iota(jnp.int32, (FB, COLS), 0)
    fold = frow == lax.broadcasted_iota(jnp.int32, (FB, COLS), 1) // SENS

    def o_copies(w):
        n = lax.rem(w, 2)
        return [
            rdma(
                oall.at[w, c_me], oall.at[w, c_me], o_send.at[n], o_recv.at[w],
                {"cells": lax.rem(c_me + j, 8)},
            )
            for j in range(1, 8)
        ]

    def dft(u, sub):
        k = lax.rem(u, CHUNKS)
        for rp in range(ROWS // 2):
            x0 = xg[k, :, 0, 2 * rp].reshape(NT, COLS)
            x1 = xg[k, :, 0, 2 * rp + 1].reshape(NT, COLS)
            both = jnp.concatenate([x0, x1], axis=1)
            v = jnp.dot(table_ref[...], both, preferred_element_type=F32).astype(BF16)
            spec[:, sub * 32 : sub * 32 + 32, rp * 256 : rp * 256 + 256] = v.reshape(GROUPS, 32, 256)

    def observe(w, lo):
        for g in range(lo, lo + GROUPS // 2):
            vg = spec[g]
            both = jnp.concatenate([gv[0, g], gv[1, g]], axis=0)
            o = lax.dot_general(vg, both, (((1,), (1,)), ((), ())), preferred_element_type=F32)
            parts = []
            for p in range(2):
                op = o[:, p * COLS : p * COLS + COLS].reshape(2 * PASS, FB, COLS)
                parts.append(jnp.sum(jnp.where(fold[None], op, 0.0), axis=1))
            a, b = parts
            rows = []
            for n in range(PASS):
                rows.append(a[2 * n : 2 * n + 1] - b[2 * n + 1 : 2 * n + 2])
                rows.append(a[2 * n + 1 : 2 * n + 2] + b[2 * n : 2 * n + 1])
            oall[w, c_me, g] = jnp.concatenate(rows, axis=0)

    def oa(w):
        observe(w, 0)

    def ob(w):
        observe(w, GROUPS // 2)
        for cp in o_copies(w):
            cp.start()

    def sib_copy(k):
        return rdma(y.at[k, other], rsib.at[k], rs_send.at[k], rs_recv.at[k, 0], sib)

    def pull(w, lo):
        for g in range(lo, lo + GROUPS // 2):
            tot = oall[w, 0, g]
            for c in range(1, 8):
                tot = tot + oall[w, c, g]
            wt = nwt[0 : 2 * PASS] * tot
            rows = []
            for n in range(PASS):
                wr = jnp.broadcast_to(wt[2 * n : 2 * n + 1], (FB, COLS))
                wi = jnp.broadcast_to(wt[2 * n + 1 : 2 * n + 2], (FB, COLS))
                wr = jnp.where(fold, wr, 0.0)
                wi = jnp.where(fold, wi, 0.0)
                rows.append(jnp.concatenate([wr, wi], axis=1))
                rows.append(jnp.concatenate([wi, -wr], axis=1))
            wm = jnp.concatenate(rows, axis=0).astype(BF16)
            for part in range(4):
                cols = slice(part * 512, part * 512 + 512)
                gg = jnp.concatenate([gv[0, g, :, cols], gv[1, g, :, cols]], axis=0)
                a = jnp.dot(wm, gg, preferred_element_type=F32).astype(BF16)
                for n in range(PASS):
                    adj[n, g * 32 : g * 32 + 32, cols] = a[n * 32 : n * 32 + 32]

    def pa(w):
        drain(oall.at[w, pl.ds(0, 7)], o_recv.at[w])
        pull(w, 0)

    def pb(w):
        pull(w, GROUPS // 2)
        drain(oall.at[w, pl.ds(0, 7)], o_send.at[lax.rem(w, 2)])

    def idft(u, sub):
        k = lax.rem(u, CHUNKS)
        for rp in range(ROWS // 2):
            v = jnp.dot(
                table_t_ref[...], adj[sub, :, rp * 256 : rp * 256 + 256], preferred_element_type=F32
            ).astype(BF16)
            for half in range(2):
                part = v[:, half * COLS : half * COLS + COLS].reshape(8, 2, STEPS, COLS)
                for c in range(2):
                    y[k, c, :, 0, 2 * rp + half] = part[:, c]
        sib_copy(k).start()

    def block(zr, dx):
        return sidx(zr, dx, 0) // 2

    def total(k, zr, dx, bb, rs, arrived):
        ci = block(zr, dx)
        tot = y[k, core, ci, bb, rs].astype(F32) + rsib[k, ci, bb, rs].astype(F32)
        for ref in arrived:
            tot = tot + ref[bb, rs].astype(F32)
        return tot

    def add_rows(k, zr, dx, lo, hi, arrived):
        for bb in range(CHUNK):
            for r in range(lo, hi, 2):
                rs = pl.ds(r, 2)
                y[k, core, block(zr, dx), bb, rs] = total(k, zr, dx, bb, rs, arrived).astype(BF16)

    def rzf_copy(k, dx):
        return rdma(
            y.at[k, core, block(1, dx), :, FIRST], rzf.at[k, dx, :, FIRST], rs_send.at[k], rs_recv.at[k, dx or 5], zp
        )

    def rxg_copy(k, zr, dx):
        i = zr * 3 + dx - 1
        return rdma(
            y.at[k, core, block(zr, dx), :, REST], rxg.at[k, i, :, REST], rs_send.at[k], rs_recv.at[k, 5 - zr], xto[dx]
        )

    def rxf_copy(k, dx):
        i = dx - 1
        return rdma(
            y.at[k, core, block(0, dx), :, FIRST], rxf.at[k, i, :, FIRST], rs_send.at[k], rs_recv.at[k, 5], xto[dx]
        )

    def rzg_copy(k):
        return rdma(
            y.at[k, core, block(1, 0), :, REST], rzg.at[k, :, REST], rs_send.at[k], rs_recv.at[k, 7], zp
        )

    def rel_copies(k):
        return [
            rdma(y.at[k, core, block(0, 2), :, rows], rel.at[k, n, :, rows], rs_send.at[k], rs_recv.at[k, 6], dev)
            for n, rows, dev in ((0, LOW, xp), (1, HIGH, xm))
        ]

    def r1(u):
        k = lax.rem(u, CHUNKS)
        sib_copy(k).wait_recv()
        add_rows(k, 0, 2, SPLIT, ROWS, ())
        for cp in rel_copies(k):
            cp.start()
        for dx in (2, 1, 3):
            add_rows(k, 1, dx, 0, SPLIT, ())
            rzf_copy(k, dx).start()
            add_rows(k, 1, dx, SPLIT, ROWS, ())
            rxg_copy(k, 1, dx).start()
        add_rows(k, 1, 0, 0, SPLIT, ())
        rzf_copy(k, 0).start()

    def r2(u):
        k = lax.rem(u, CHUNKS)
        for dx in (2, 1, 3):
            rzf_copy(k, dx).wait_recv()
            add_rows(k, 0, dx, 0, SPLIT, (rzf.at[k, dx],))
            rxf_copy(k, dx).start()
        drain(rxg.at[k, pl.ds(3, 3), :, REST], rs_recv.at[k, 4])
        add_rows(k, 1, 0, SPLIT, ROWS, [rxg.at[k, 3 + i] for i in range(3)])
        rzg_copy(k).start()
        drain(rel.at[k, 0, :, REST], rs_recv.at[k, 6])
        mid = SPLIT + 4
        add_rows(k, 0, 1, SPLIT, mid, (rel.at[k, 0],))
        add_rows(k, 0, 1, mid, ROWS, ())
        rxg_copy(k, 0, 1).start()
        add_rows(k, 0, 3, SPLIT, mid, ())
        add_rows(k, 0, 3, mid, ROWS, (rel.at[k, 1],))
        rxg_copy(k, 0, 3).start()

    def r3(u):
        k = lax.rem(u, CHUNKS)
        drain(rxg.at[k, pl.ds(0, 3)], rs_recv.at[k, 5])
        rzg_copy(k).wait_recv()
        for bb in range(CHUNK):
            b = k * CHUNK + bb
            for i in range(0, ROWS, 2):
                er = pl.ds(HALO + i, 2)
                rs = pl.ds(i, 2)
                us = [c_s[HALO + i - 1 + n] * xf[b, i + n] for n in range(4)]
                if i < SPLIT:
                    arrived = [rzf.at[k, 0]] + [rxf.at[k, n] for n in range(3)]
                else:
                    arrived = [rzg.at[k]] + [rxg.at[k, n] for n in (0, 2)]
                m = total(k, 0, 0, bb, rs, arrived)
                for n in range(2):
                    e = HALO + i + n
                    nb = us[n] + us[n + 2] + sides(us[n + 1])
                    prior = c_d[e] * xf[b, i + n + 1] - c_s[e] * nb
                    r = rhs_ext[b, e] - (prior + m[n])
                    res_ext[b, e] = r
                    put_rows(res_ref, b, i + n, r)
        halo_start(res_ext, 1, k)

        @pl.when(u >= CHUNKS)
        def _():
            pltpu.make_async_copy(res_ref.at[:, k], res_out.at[:, k], out_sem.at[1]).start()

        drain(xg.at[k, pl.ds(0, 15)], rs_send.at[k])

    def own_to_gather(k):
        for bb in range(CHUNK):
            b = k * CHUNK + bb

            def body(i, carry, b=b, bb=bb):
                xg[k, d_me, bb, pl.ds(i * 4, 4)] = xf[b, pl.ds(1 + i * 4, 4)].astype(BF16)
                return carry

            lax.fori_loop(0, ROWS // 4, body, 0, unroll=4)

    def begin(k):
        halo_finish(rhs_ext, 0, k)
        for bb in range(CHUNK):
            b = k * CHUNK + bb
            precondition(rhs_ext, b, 0)

    def update(k, mode):
        halo_finish(res_ext, 1, k)

        for bb in range(CHUNK):
            precondition(res_ext, k * CHUNK + bb, mode)
        if mode == 2:
            pltpu.make_async_copy(sol_ref.at[:, k], sol_out.at[:, k], out_sem.at[0]).start()

    def finish_map():
        drain(gv, loc_sem.at[6])

        def body(i, carry):
            rs = pl.ds(pl.multiple_of(lax.rem(i, 8) * 16, 16), 16)
            g = i // 8
            gv[0, g, rs] = gv[0, g, rs] + marks[...]
            return carry

        lax.fori_loop(0, 64, body, 0, unroll=4)

    def advance(u):
        @pl.when(u < CHUNKS)
        def _():
            begin(u)

        @pl.when(jnp.logical_and(u >= CHUNKS, u < JOBS))
        def _():
            update(lax.rem(u, CHUNKS), 1)

        @pl.when(u >= JOBS)
        def _():
            update(lax.rem(u, CHUNKS), 2)

    stages = {"a0": a0, "a1": a1, "a2": a2, "a3": a3, "r1": r1, "r2": r2, "r3": r3}
    sampled = {"dft": dft, "idft": idft}
    passes = {"oa": oa, "ob": ob, "pa": pa, "pb": pb}

    def step(t, carry):
        for name, sub, late in ORDER:
            w = t - late

            def run(name=name, sub=sub, w=w):
                if name == "update":
                    advance(w * PASS + sub)
                elif name in stages:
                    stages[name](w * PASS + sub)
                elif name in sampled:
                    sampled[name](w * PASS + sub, sub)
                else:
                    passes[name](w)

            last = PASSES + PASSES // 2 if name == "update" else PASSES
            pl.when(jnp.logical_and(w >= 0, w < last))(run)
            if name == "a0" and sub == PASS - 1:
                pl.when(t == 0)(finish_map)
        return carry

    lax.fori_loop(0, PASSES + PASSES // 2, step, 0)
    drain(sol_ref, out_sem.at[0])
    drain(res_ref, out_sem.at[1])


def write_out(a_ref, b_ref, a_out, b_out, sem):
    copies = [
        pltpu.make_async_copy(a_ref, a_out, sem.at[0]),
        pltpu.make_async_copy(b_ref, b_out, sem.at[1]),
    ]
    for cp in copies:
        cp.start()
    for cp in copies:
        cp.wait()


def shards(rhs, forward_map, stiffness, reaction, noise_weight, sensor_cell):
    table = transform_tables()
    maps = forward_map.reshape(2, GROUPS, FB * SENS, CELLS)
    vm = pl.BlockSpec(memory_space=pltpu.VMEM)
    sm = pl.BlockSpec(memory_space=pltpu.SMEM)
    hb = pl.BlockSpec(memory_space=pl.ANY)
    block = (CHUNK, ROWS, STEPS, COLS)
    dma = pltpu.SemaphoreType.DMA
    out = jax.ShapeDtypeStruct((STEPS, 6, ROWS, COLS), F32)
    scratch = [
        pltpu.VMEM((2, GROUPS, FB * SENS, CELLS), BF16),
        pltpu.VMEM((CHUNKS, 16) + block, BF16),
        pltpu.VMEM((GROUPS, 32 * PASS, CELLS), BF16),
        pltpu.VMEM((PASS, NT, CELLS), BF16),
        pltpu.VMEM((CHUNKS, 2, 8) + block, BF16),
        pltpu.VMEM((CHUNKS, 8) + block, BF16),
        pltpu.VMEM((CHUNKS, 4) + block, BF16),
        pltpu.VMEM((CHUNKS, 6) + block, BF16),
        pltpu.VMEM((CHUNKS, 3) + block, BF16),
        pltpu.VMEM((CHUNKS, 2) + block, BF16),
        pltpu.VMEM((CHUNKS,) + block, BF16),
        pltpu.VMEM((PASSES, 8, GROUPS, 2 * PASS, COLS), F32),
        pltpu.VMEM((6, EXT, STEPS, COLS), F32),
        pltpu.VMEM((6, EXT, STEPS, COLS), F32),
        pltpu.VMEM((2, CHUNKS, 2, HALO, STEPS, COLS), BF16),
        pltpu.VMEM((2, CHUNKS, 2, HALO, STEPS, COLS), BF16),
        pltpu.VMEM((6, STEPS, ROWS, COLS), F32),
        pltpu.VMEM((6, ROWS + 2, STEPS, COLS), F32),
        pltpu.VMEM((32, COLS), F32),
        pltpu.VMEM((32, COLS), F32),
        pltpu.VMEM((4, 8, COLS), F32),
        pltpu.VMEM((EXT, STEPS, COLS), F32),
        pltpu.VMEM((EXT, STEPS, COLS), F32),
        pltpu.VMEM((EXT, STEPS, COLS), F32),
        pltpu.VMEM((EXT, STEPS, COLS), F32),
        pltpu.VMEM((EXT, STEPS, COLS), F32),
        pltpu.VMEM((16, CELLS), BF16),
        pltpu.VMEM((8, COLS), F32),
        pltpu.VMEM((STEPS, 6, ROWS, COLS), F32),
        pltpu.VMEM((STEPS, 6, ROWS, COLS), F32),
        dma((2,)),
        dma((7,)),
        dma((2,)),
        dma((CHUNKS,)),
        dma((CHUNKS, 7)),
        dma((CHUNKS,)),
        dma((CHUNKS, 8)),
        dma((2,)),
        dma((PASSES,)),
        dma((2, CHUNKS)),
        dma((2, CHUNKS)),
    ]
    sol, res = pl.pallas_call(
        kernel,
        out_shape=(out, out),
        in_specs=[hb, hb, vm, vm, sm, sm, vm, vm],
        out_specs=(hb, hb),
        scratch_shapes=scratch,
        compiler_params=pltpu.CompilerParams(
            collective_id=0, has_side_effects=True, vmem_limit_bytes=60 * 1024 * 1024
        ),
    )(
        rhs,
        maps,
        stiffness,
        reaction,
        noise_weight,
        sensor_cell,
        jnp.asarray(table, BF16),
        jnp.asarray(table.T, BF16),
    )
    place = pl.BlockSpec(memory_space=pl.ANY)
    return pl.pallas_call(
        write_out,
        out_shape=(out, out),
        in_specs=[vm, vm],
        out_specs=(place, place),
        scratch_shapes=[dma((2,))],
    )(sol, res)


def solution(mesh):
    placed = (
        P("sensors", None, "cells", None),
        P(None, None, "sensors", "cells"),
        P("cells", None),
        P("cells", None),
        P(),
        P(),
    )
    return jax.shard_map(
        shards,
        mesh=mesh,
        in_specs=placed,
        out_specs=(P("sensors", None, "cells", None), P("sensors", None, "cells", None)),
        check_vma=False,
    )
```

```python
import functools
import math

import jax
import jax.numpy as jnp
import numpy as np
from jax import lax
from jax.experimental import pallas as pl
from jax.experimental.pallas import tpu as pltpu
from jax.sharding import PartitionSpec as P

MESH = pl.DeviceIdType.MESH
BF16 = jnp.bfloat16
F32 = jnp.float32
DAMPING = 0.8
ROWS = 16
HALO = 4
EXT = ROWS + 2 * HALO
STEPS = 16
COLS = 128
CELLS = ROWS * COLS
NT = 256
FB = 16
GROUPS = 8
SENS = 8
CHUNK = 1
CHUNKS = 6 // CHUNK
SPLIT = 8
FIRST = pl.ds(0, SPLIT)
REST = pl.ds(SPLIT, ROWS - SPLIT)
LOW = pl.ds(SPLIT, 4)
HIGH = pl.ds(SPLIT + 4, 4)
PASS = 2
PASSES = 12 // PASS
ORDER = (
    ("update", 0, 0),
    ("a0", 0, 0),
    ("a2", 0, 1),
    ("idft", 1, 2),
    ("r1", 0, 2),
    ("a3", 0, 1),
    ("a2", 1, 1),
    ("dft", 0, 1),
    ("r1", 1, 2),
    ("a3", 1, 1),
    ("dft", 1, 1),
    ("oa", 0, 1),
    ("ob", 0, 1),
    ("r2", 0, 2),
    ("update", 1, 0),
    ("a0", 1, 0),
    ("r2", 1, 2),
    ("a1", 0, 0),
    ("r3", 0, 2),
    ("pa", 0, 1),
    ("a1", 1, 0),
    ("pb", 0, 1),
    ("idft", 0, 1),
    ("r3", 1, 2),
)
JOBS = 2 * CHUNKS


def transform_tables():
    wave = np.arange(128)[:, None]
    moment = np.arange(NT)[None, :]
    phase = (wave * moment % NT).astype(np.float32) * np.float32(2.0 * math.pi / NT)
    factor = np.float32(1.0 / math.sqrt(NT))
    real = (np.cos(phase) * factor).reshape(GROUPS, 1, FB, NT)
    imag = (-np.sin(phase) * factor).reshape(GROUPS, 1, FB, NT)
    return np.concatenate([real, imag], axis=1).reshape(NT, NT)


def kernel(
    rhs_hbm,
    map_hbm,
    stiff_ref,
    react_ref,
    weight_sm,
    cell_sm,
    table_ref,
    table_t_ref,
    sol_out,
    res_out,
    gv,
    xg,
    spec,
    adj,
    y,
    rsib,
    rzf,
    rxg,
    rxf,
    rel,
    rzg,
    oall,
    rhs_ext,
    res_ext,
    hin,
    hout,
    stage,
    xf,
    sx,
    qx,
    sxin,
    c_sw,
    c_k,
    c_s,
    c_si,
    c_d,
    marks,
    nwt,
    sol_ref,
    res_ref,
    out_sem,
    loc_sem,
    init_sem,
    ag_send,
    ag_recv,
    rs_send,
    rs_recv,
    o_send,
    o_recv,
    halo_send,
    halo_recv,
):
    c_me = lax.axis_index("cells")
    s_me = lax.axis_index("sensors")
    core = lax.rem(s_me, 2)
    chip = s_me // 2
    xpos = lax.rem(chip, 4)
    zpos = chip // 4

    def sidx(dz, dx, cc):
        return (lax.rem(zpos + dz, 2) * 4 + lax.rem(xpos + dx, 4)) * 2 + cc

    other = 1 - core
    sib = {"sensors": sidx(0, 0, other)}
    xp = {"sensors": sidx(0, 1, core)}
    xm = {"sensors": sidx(0, 3, core)}
    zp = {"sensors": sidx(1, 0, core)}
    xd = {"sensors": sidx(0, 2, core)}
    xto = {1: xp, 2: xd, 3: xm}
    cnext = {"cells": lax.rem(c_me + 1, 8)}
    cprev = {"cells": lax.rem(c_me + 7, 8)}

    def rdma(src, dst, ss, rs, dev):
        return pltpu.make_async_remote_copy(
            src_ref=src, dst_ref=dst, send_sem=ss, recv_sem=rs, device_id=dev, device_id_type=MESH
        )

    def drain(ref, sem):
        pltpu.make_async_copy(ref, ref, sem).wait()

    map_copies = [
        pltpu.make_async_copy(map_hbm.at[p, g], gv.at[p, g], loc_sem.at[6])
        for p in range(2)
        for g in range(GROUPS)
    ]
    rhs_copies = [
        pltpu.make_async_copy(
            rhs_hbm.at[:, b], stage.at[b], loc_sem.at[b]
        )
        for b in range(6)
    ]
    for cp in rhs_copies:
        cp.start()
    for cp in map_copies:
        cp.start()

    barrier = pltpu.get_barrier_semaphore()
    peers = [sib, xp, xm, xd, zp] + [{"cells": lax.rem(c_me + j, 8)} for j in range(1, 8)]
    for peer in peers:
        pl.semaphore_signal(barrier, inc=1, device_id=peer, device_id_type=MESH)

    def coef_copies():
        return [
            rdma(stiff_ref.at[pl.ds(8, 8)], sxin.at[0], init_sem.at[0], init_sem.at[1], cnext),
            rdma(stiff_ref.at[pl.ds(0, 8)], sxin.at[1], init_sem.at[0], init_sem.at[1], cprev),
            rdma(react_ref.at[pl.ds(8, 8)], sxin.at[2], init_sem.at[0], init_sem.at[1], cnext),
            rdma(react_ref.at[pl.ds(0, 8)], sxin.at[3], init_sem.at[0], init_sem.at[1], cprev),
        ]

    def halo_start(ref, phase, k):
        for n, lo, dev in ((0, ROWS, cnext), (1, HALO, cprev)):
            hout[phase, k, n] = ref[k, pl.ds(lo, HALO)].astype(BF16)
            rdma(hout.at[phase, k, n], hin.at[phase, k, n], halo_send.at[phase, k], halo_recv.at[phase, k], dev).start()

    def halo_finish(ref, phase, k):
        drain(hin.at[phase, k], halo_recv.at[phase, k])
        drain(hout.at[phase, k], halo_send.at[phase, k])
        for n, lo in ((0, 0), (1, HALO + ROWS)):
            ref[k, pl.ds(lo, HALO)] = hin[phase, k, n].astype(F32)

    for b in range(6):
        rhs_copies[b].wait()
        flat = stage.at[b].reshape(STEPS * ROWS, COLS)
        for r in range(ROWS):
            rhs_ext[b, HALO + r] = flat[pl.ds(r, STEPS, stride=ROWS), :]

    lane = lax.broadcasted_iota(jnp.int32, (8, COLS), 1)
    acc = jnp.zeros((8, COLS), F32)
    for s in range(SENS):
        acc = jnp.where(lax.rem(lane, 8) == s, weight_sm[s_me * SENS + s], acc)
    nwt[...] = acc
    row = lax.broadcasted_iota(jnp.int32, (16, 512), 0)
    target = jnp.zeros((16, 512), jnp.int32)
    for s in range(SENS):
        target = jnp.where(lax.rem(row, 8) == s, cell_sm[s_me * SENS + s], target)
    for part in range(4):
        cell_id = lax.broadcasted_iota(jnp.int32, (16, 512), 1) + (c_me * CELLS + part * 512)
        marks[:, part * 512 : (part + 1) * 512] = jnp.where(cell_id == target, 1.0, 0.0).astype(BF16)

    pl.semaphore_wait(barrier, len(peers))
    for cp in coef_copies():
        cp.start()
    for b in range(6):
        halo_start(rhs_ext, 0, b)

    sx[8:24, :] = stiff_ref[...]
    qx[8:24, :] = react_ref[...]
    drain(sxin, init_sem.at[0])
    drain(sxin, init_sem.at[1])
    sx[0:8, :] = sxin[0]
    sx[24:32, :] = sxin[1]
    qx[0:8, :] = sxin[2]
    qx[24:32, :] = sxin[3]
    erow = lax.broadcasted_iota(jnp.int32, (32, COLS), 0) + (c_me * ROWS - 8)
    inside = jnp.logical_and(erow >= 0, erow < 128)
    st = jnp.where(inside, sx[...], 0.0)
    re = jnp.where(inside, qx[...], 1.0)
    dg = re + 4.0 * st * st
    wv = DAMPING / dg
    si = jnp.where(inside, 1.0 / jnp.where(inside, st, 1.0), 0.0)
    for ref, val in ((c_sw, st * wv), (c_k, st * st * wv), (c_s, st), (c_si, si), (c_d, dg)):
        ref[...] = jnp.broadcast_to(val[8 - HALO : 8 - HALO + EXT][:, None, :], (EXT, STEPS, COLS))

    lane_s = lax.broadcasted_iota(jnp.int32, (STEPS, COLS), 1)
    not_first = lane_s > 0
    not_last = lane_s < COLS - 1

    def put_rows(ref, b, r, value):
        ref.reshape(STEPS * 6 * ROWS, COLS)[pl.ds(b * ROWS + r, STEPS, stride=6 * ROWS), :] = value

    def sides(v):
        left = pltpu.roll(v, 1, 1)
        right = pltpu.roll(v, COLS - 1, 1)
        return jnp.where(not_first, left, 0.0) + jnp.where(not_last, right, 0.0)

    def precondition(src, b, mode):
        levels = [{}, {}, {}]
        first = {}
        for r in range(EXT + 3):
            if r < EXT:
                first[r] = c_sw[r] * src[b, r]
                levels[0][r] = first[r]
            for n in range(3):
                q = r - 1 - n
                if not n + 1 <= q <= EXT - 2 - n:
                    continue
                now = levels[n]
                nb = now[q - 1] + now[q + 1] + sides(now[q])
                new = (1.0 - DAMPING) * now[q] + first[q] + c_k[q] * nb
                if n < 2:
                    levels[n + 1][q] = new
                elif mode == 0:
                    xf[b, q - 3] = c_si[q] * new
                elif mode == 1:
                    xf[b, q - 3] = xf[b, q - 3] + c_si[q] * new
                elif HALO <= q < HALO + ROWS:
                    put_rows(sol_ref, b, q - HALO, xf[b, q - 3] + c_si[q] * new)

    d_me = s_me

    def ag_copy(k, idx, dz, dx, rows, dev):
        d = sidx(dz, dx, core)
        ref = xg.at[k, d] if rows is None else xg.at[k, d, :, rows]
        which = {1: 0, 2: 1, 3: 2, 4: 3, 18: 6, 19: 6}.get(idx, 4 if 5 <= idx <= 10 else 5)
        return rdma(ref, ref, ag_send.at[k], ag_recv.at[k, which], dev)

    def ag_copies(k):
        table = [
            (0, 0, None, sib),
            (0, 0, None, xp),
            (0, 0, None, xm),
            (0, 0, FIRST, xd),
            (0, 0, None, zp),
            (1, 0, REST, xp),
            (1, 0, REST, xm),
            (1, 0, REST, xd),
            (0, 3, FIRST, zp),
            (0, 1, FIRST, zp),
            (0, 2, FIRST, zp),
            (0, 3, None, sib),
            (0, 1, None, sib),
            (0, 2, None, sib),
            (1, 0, None, sib),
            (1, 3, None, sib),
            (1, 1, None, sib),
            (1, 2, None, sib),
            (0, 3, LOW, xp),
            (0, 1, HIGH, xm),
        ]
        return [ag_copy(k, i, *row) for i, row in enumerate(table)]

    def a0(u):
        k = lax.rem(u, CHUNKS)
        own_to_gather(k)
        s = ag_copies(k)
        for i in (4, 1, 2, 3, 0):
            s[i].start()

    def a1(u):
        s = ag_copies(lax.rem(u, CHUNKS))
        s[4].wait_recv()
        for i in (5, 6, 7, 14):
            s[i].start()
        for i, more in ((1, (18, 8, 11)), (2, (19, 9, 12)), (3, (10,))):
            s[i].wait_recv()
            for n in more:
                s[n].start()

    def a2(u):
        k = lax.rem(u, CHUNKS)
        s = ag_copies(k)
        drain(xg.at[k, 0, :, REST], ag_recv.at[k, 6])
        s[13].start()
        drain(xg.at[k, pl.ds(0, 3)], ag_recv.at[k, 4])
        for f in (15, 16, 17):
            s[f].start()

    def a3(u):
        k = lax.rem(u, CHUNKS)
        drain(xg.at[k, pl.ds(0, 8)], ag_recv.at[k, 5])
        drain(xg.at[k, pl.ds(0, 15)], ag_send.at[k])

    frow = lax.broadcasted_iota(jnp.int32, (FB, COLS), 0)
    fold = frow == lax.broadcasted_iota(jnp.int32, (FB, COLS), 1) // SENS

    def o_copies(w):
        n = lax.rem(w, 2)
        return [
            rdma(
                oall.at[w, c_me], oall.at[w, c_me], o_send.at[n], o_recv.at[w],
                {"cells": lax.rem(c_me + j, 8)},
            )
            for j in range(1, 8)
        ]

    def dft(u, sub):
        k = lax.rem(u, CHUNKS)
        for rp in range(ROWS // 2):
            x0 = xg[k, :, 0, 2 * rp].reshape(NT, COLS)
            x1 = xg[k, :, 0, 2 * rp + 1].reshape(NT, COLS)
            both = jnp.concatenate([x0, x1], axis=1)
            v = jnp.dot(table_ref[...], both, preferred_element_type=F32).astype(BF16)
            spec[:, sub * 32 : sub * 32 + 32, rp * 256 : rp * 256 + 256] = v.reshape(GROUPS, 32, 256)

    def observe(w, lo):
        for g in range(lo, lo + GROUPS // 2):
            vg = spec[g]
            both = jnp.concatenate([gv[0, g], gv[1, g]], axis=0)
            o = lax.dot_general(vg, both, (((1,), (1,)), ((), ())), preferred_element_type=F32)
            parts = []
            for p in range(2):
                op = o[:, p * COLS : p * COLS + COLS].reshape(2 * PASS, FB, COLS)
                parts.append(jnp.sum(jnp.where(fold[None], op, 0.0), axis=1))
            a, b = parts
            rows = []
            for n in range(PASS):
                rows.append(a[2 * n : 2 * n + 1] - b[2 * n + 1 : 2 * n + 2])
                rows.append(a[2 * n + 1 : 2 * n + 2] + b[2 * n : 2 * n + 1])
            oall[w, c_me, g] = jnp.concatenate(rows, axis=0)

    def oa(w):
        observe(w, 0)

    def ob(w):
        observe(w, GROUPS // 2)
        for cp in o_copies(w):
            cp.start()

    def sib_copy(k):
        return rdma(y.at[k, other], rsib.at[k], rs_send.at[k], rs_recv.at[k, 0], sib)

    def pull(w, lo):
        for g in range(lo, lo + GROUPS // 2):
            tot = oall[w, 0, g]
            for c in range(1, 8):
                tot = tot + oall[w, c, g]
            wt = nwt[0 : 2 * PASS] * tot
            rows = []
            for n in range(PASS):
                wr = jnp.broadcast_to(wt[2 * n : 2 * n + 1], (FB, COLS))
                wi = jnp.broadcast_to(wt[2 * n + 1 : 2 * n + 2], (FB, COLS))
                wr = jnp.where(fold, wr, 0.0)
                wi = jnp.where(fold, wi, 0.0)
                rows.append(jnp.concatenate([wr, wi], axis=1))
                rows.append(jnp.concatenate([wi, -wr], axis=1))
            wm = jnp.concatenate(rows, axis=0).astype(BF16)
            for part in range(4):
                cols = slice(part * 512, part * 512 + 512)
                gg = jnp.concatenate([gv[0, g, :, cols], gv[1, g, :, cols]], axis=0)
                a = jnp.dot(wm, gg, preferred_element_type=F32).astype(BF16)
                for n in range(PASS):
                    adj[n, g * 32 : g * 32 + 32, cols] = a[n * 32 : n * 32 + 32]

    def pa(w):
        drain(oall.at[w, pl.ds(0, 7)], o_recv.at[w])
        pull(w, 0)

    def pb(w):
        pull(w, GROUPS // 2)
        drain(oall.at[w, pl.ds(0, 7)], o_send.at[lax.rem(w, 2)])

    def idft(u, sub):
        k = lax.rem(u, CHUNKS)
        for rp in range(ROWS // 2):
            v = jnp.dot(
                table_t_ref[...], adj[sub, :, rp * 256 : rp * 256 + 256], preferred_element_type=F32
            ).astype(BF16)
            for half in range(2):
                part = v[:, half * COLS : half * COLS + COLS].reshape(8, 2, STEPS, COLS)
                for c in range(2):
                    y[k, c, :, 0, 2 * rp + half] = part[:, c]
        sib_copy(k).start()

    def block(zr, dx):
        return sidx(zr, dx, 0) // 2

    def total(k, zr, dx, bb, rs, arrived):
        ci = block(zr, dx)
        tot = y[k, core, ci, bb, rs].astype(F32) + rsib[k, ci, bb, rs].astype(F32)
        for ref in arrived:
            tot = tot + ref[bb, rs].astype(F32)
        return tot

    def add_rows(k, zr, dx, lo, hi, arrived):
        for bb in range(CHUNK):
            for r in range(lo, hi, 2):
                rs = pl.ds(r, 2)
                y[k, core, block(zr, dx), bb, rs] = total(k, zr, dx, bb, rs, arrived).astype(BF16)

    def rzf_copy(k, dx):
        return rdma(
            y.at[k, core, block(1, dx), :, FIRST], rzf.at[k, dx, :, FIRST], rs_send.at[k], rs_recv.at[k, dx or 5], zp
        )

    def rxg_copy(k, zr, dx):
        i = zr * 3 + dx - 1
        return rdma(
            y.at[k, core, block(zr, dx), :, REST], rxg.at[k, i, :, REST], rs_send.at[k], rs_recv.at[k, 5 - zr], xto[dx]
        )

    def rxf_copy(k, dx):
        i = dx - 1
        return rdma(
            y.at[k, core, block(0, dx), :, FIRST], rxf.at[k, i, :, FIRST], rs_send.at[k], rs_recv.at[k, 5], xto[dx]
        )

    def rzg_copy(k):
        return rdma(
            y.at[k, core, block(1, 0), :, REST], rzg.at[k, :, REST], rs_send.at[k], rs_recv.at[k, 7], zp
        )

    def rel_copies(k):
        return [
            rdma(y.at[k, core, block(0, 2), :, rows], rel.at[k, n, :, rows], rs_send.at[k], rs_recv.at[k, 6], dev)
            for n, rows, dev in ((0, LOW, xp), (1, HIGH, xm))
        ]

    def r1(u):
        k = lax.rem(u, CHUNKS)
        sib_copy(k).wait_recv()
        add_rows(k, 0, 2, SPLIT, ROWS, ())
        for cp in rel_copies(k):
            cp.start()
        for dx in (2, 1, 3):
            add_rows(k, 1, dx, 0, SPLIT, ())
            rzf_copy(k, dx).start()
            add_rows(k, 1, dx, SPLIT, ROWS, ())
            rxg_copy(k, 1, dx).start()
        add_rows(k, 1, 0, 0, SPLIT, ())
        rzf_copy(k, 0).start()

    def r2(u):
        k = lax.rem(u, CHUNKS)
        for dx in (2, 1, 3):
            rzf_copy(k, dx).wait_recv()
            add_rows(k, 0, dx, 0, SPLIT, (rzf.at[k, dx],))
            rxf_copy(k, dx).start()
        drain(rxg.at[k, pl.ds(3, 3), :, REST], rs_recv.at[k, 4])
        add_rows(k, 1, 0, SPLIT, ROWS, [rxg.at[k, 3 + i] for i in range(3)])
        rzg_copy(k).start()
        drain(rel.at[k, 0, :, REST], rs_recv.at[k, 6])
        mid = SPLIT + 4
        add_rows(k, 0, 1, SPLIT, mid, (rel.at[k, 0],))
        add_rows(k, 0, 1, mid, ROWS, ())
        rxg_copy(k, 0, 1).start()
        add_rows(k, 0, 3, SPLIT, mid, ())
        add_rows(k, 0, 3, mid, ROWS, (rel.at[k, 1],))
        rxg_copy(k, 0, 3).start()

    def r3(u):
        k = lax.rem(u, CHUNKS)
        drain(rxg.at[k, pl.ds(0, 3)], rs_recv.at[k, 5])
        rzg_copy(k).wait_recv()
        for bb in range(CHUNK):
            b = k * CHUNK + bb
            for i in range(0, ROWS, 2):
                er = pl.ds(HALO + i, 2)
                rs = pl.ds(i, 2)
                us = [c_s[HALO + i - 1 + n] * xf[b, i + n] for n in range(4)]
                if i < SPLIT:
                    arrived = [rzf.at[k, 0]] + [rxf.at[k, n] for n in range(3)]
                else:
                    arrived = [rzg.at[k]] + [rxg.at[k, n] for n in (0, 2)]
                m = total(k, 0, 0, bb, rs, arrived)
                for n in range(2):
                    e = HALO + i + n
                    nb = us[n] + us[n + 2] + sides(us[n + 1])
                    prior = c_d[e] * xf[b, i + n + 1] - c_s[e] * nb
                    r = rhs_ext[b, e] - (prior + m[n])
                    res_ext[b, e] = r
                    put_rows(res_ref, b, i + n, r)
        halo_start(res_ext, 1, k)

        @pl.when(u >= CHUNKS)
        def _():
            pltpu.make_async_copy(res_ref.at[:, k], res_out.at[:, k], out_sem.at[1]).start()

        drain(xg.at[k, pl.ds(0, 15)], rs_send.at[k])

    def own_to_gather(k):
        for bb in range(CHUNK):
            b = k * CHUNK + bb

            def body(i, carry, b=b, bb=bb):
                xg[k, d_me, bb, pl.ds(i * 4, 4)] = xf[b, pl.ds(1 + i * 4, 4)].astype(BF16)
                return carry

            lax.fori_loop(0, ROWS // 4, body, 0, unroll=4)

    def begin(k):
        halo_finish(rhs_ext, 0, k)
        for bb in range(CHUNK):
            b = k * CHUNK + bb
            precondition(rhs_ext, b, 0)

    def update(k, mode):
        halo_finish(res_ext, 1, k)

        for bb in range(CHUNK):
            precondition(res_ext, k * CHUNK + bb, mode)
        if mode == 2:
            pltpu.make_async_copy(sol_ref.at[:, k], sol_out.at[:, k], out_sem.at[0]).start()

    def finish_map():
        drain(gv, loc_sem.at[6])

        def body(i, carry):
            rs = pl.ds(pl.multiple_of(lax.rem(i, 8) * 16, 16), 16)
            g = i // 8
            gv[0, g, rs] = gv[0, g, rs] + marks[...]
            return carry

        lax.fori_loop(0, 64, body, 0, unroll=4)

    def advance(u):
        @pl.when(u < CHUNKS)
        def _():
            begin(u)

        @pl.when(jnp.logical_and(u >= CHUNKS, u < JOBS))
        def _():
            update(lax.rem(u, CHUNKS), 1)

        @pl.when(u >= JOBS)
        def _():
            update(lax.rem(u, CHUNKS), 2)

    stages = {"a0": a0, "a1": a1, "a2": a2, "a3": a3, "r1": r1, "r2": r2, "r3": r3}
    sampled = {"dft": dft, "idft": idft}
    passes = {"oa": oa, "ob": ob, "pa": pa, "pb": pb}

    def step(t, carry):
        for name, sub, late in ORDER:
            w = t - late

            def run(name=name, sub=sub, w=w):
                if name == "update":
                    advance(w * PASS + sub)
                elif name in stages:
                    stages[name](w * PASS + sub)
                elif name in sampled:
                    sampled[name](w * PASS + sub, sub)
                else:
                    passes[name](w)

            last = PASSES + PASSES // 2 if name == "update" else PASSES
            pl.when(jnp.logical_and(w >= 0, w < last))(run)
            if name == "a0" and sub == PASS - 1:
                pl.when(t == 0)(finish_map)
        return carry

    lax.fori_loop(0, PASSES + PASSES // 2, step, 0)
    drain(sol_ref, out_sem.at[0])
    drain(res_ref, out_sem.at[1])


def write_out(a_ref, b_ref, a_out, b_out, sem):
    copies = [
        pltpu.make_async_copy(a_ref, a_out, sem.at[0]),
        pltpu.make_async_copy(b_ref, b_out, sem.at[1]),
    ]
    for cp in copies:
        cp.start()
    for cp in copies:
        cp.wait()


def shards(rhs, forward_map, stiffness, reaction, noise_weight, sensor_cell):
    table = transform_tables()
    maps = forward_map.reshape(2, GROUPS, FB * SENS, CELLS)
    vm = pl.BlockSpec(memory_space=pltpu.VMEM)
    sm = pl.BlockSpec(memory_space=pltpu.SMEM)
    hb = pl.BlockSpec(memory_space=pl.ANY)
    block = (CHUNK, ROWS, STEPS, COLS)
    dma = pltpu.SemaphoreType.DMA
    out = jax.ShapeDtypeStruct((STEPS, 6, ROWS, COLS), F32)
    scratch = [
        pltpu.VMEM((2, GROUPS, FB * SENS, CELLS), BF16),
        pltpu.VMEM((CHUNKS, 16) + block, BF16),
        pltpu.VMEM((GROUPS, 32 * PASS, CELLS), BF16),
        pltpu.VMEM((PASS, NT, CELLS), BF16),
        pltpu.VMEM((CHUNKS, 2, 8) + block, BF16),
        pltpu.VMEM((CHUNKS, 8) + block, BF16),
        pltpu.VMEM((CHUNKS, 4) + block, BF16),
        pltpu.VMEM((CHUNKS, 6) + block, BF16),
        pltpu.VMEM((CHUNKS, 3) + block, BF16),
        pltpu.VMEM((CHUNKS, 2) + block, BF16),
        pltpu.VMEM((CHUNKS,) + block, BF16),
        pltpu.VMEM((PASSES, 8, GROUPS, 2 * PASS, COLS), F32),
        pltpu.VMEM((6, EXT, STEPS, COLS), F32),
        pltpu.VMEM((6, EXT, STEPS, COLS), F32),
        pltpu.VMEM((2, CHUNKS, 2, HALO, STEPS, COLS), BF16),
        pltpu.VMEM((2, CHUNKS, 2, HALO, STEPS, COLS), BF16),
        pltpu.VMEM((6, STEPS, ROWS, COLS), F32),
        pltpu.VMEM((6, ROWS + 2, STEPS, COLS), F32),
        pltpu.VMEM((32, COLS), F32),
        pltpu.VMEM((32, COLS), F32),
        pltpu.VMEM((4, 8, COLS), F32),
        pltpu.VMEM((EXT, STEPS, COLS), F32),
        pltpu.VMEM((EXT, STEPS, COLS), F32),
        pltpu.VMEM((EXT, STEPS, COLS), F32),
        pltpu.VMEM((EXT, STEPS, COLS), F32),
        pltpu.VMEM((EXT, STEPS, COLS), F32),
        pltpu.VMEM((16, CELLS), BF16),
        pltpu.VMEM((8, COLS), F32),
        pltpu.VMEM((STEPS, 6, ROWS, COLS), F32),
        pltpu.VMEM((STEPS, 6, ROWS, COLS), F32),
        dma((2,)),
        dma((7,)),
        dma((2,)),
        dma((CHUNKS,)),
        dma((CHUNKS, 7)),
        dma((CHUNKS,)),
        dma((CHUNKS, 8)),
        dma((2,)),
        dma((PASSES,)),
        dma((2, CHUNKS)),
        dma((2, CHUNKS)),
    ]
    sol, res = pl.pallas_call(
        kernel,
        out_shape=(out, out),
        in_specs=[hb, hb, vm, vm, sm, sm, vm, vm],
        out_specs=(hb, hb),
        scratch_shapes=scratch,
        compiler_params=pltpu.CompilerParams(
            collective_id=0, has_side_effects=True, vmem_limit_bytes=60 * 1024 * 1024
        ),
    )(
        rhs,
        maps,
        stiffness,
        reaction,
        noise_weight,
        sensor_cell,
        jnp.asarray(table, BF16),
        jnp.asarray(table.T, BF16),
    )
    place = pl.BlockSpec(memory_space=pl.ANY)
    return pl.pallas_call(
        write_out,
        out_shape=(out, out),
        in_specs=[vm, vm],
        out_specs=(place, place),
        scratch_shapes=[dma((2,))],
    )(sol, res)


def solution(mesh):
    placed = (
        P("sensors", None, "cells", None),
        P(None, None, "sensors", "cells"),
        P("cells", None),
        P("cells", None),
        P(),
        P(),
    )
    return jax.shard_map(
        shards,
        mesh=mesh,
        in_specs=placed,
        out_specs=(P("sensors", None, "cells", None), P("sensors", None, "cells", None)),
        check_vma=False,
    )
```
